256 devices in a mesh: aa: 4 (over x), ba: 8 (over z), col: 8 (over y, core).
Axes of the slice: x: 4, y: 4, z: 8, core: 2. Of those that a mesh axis runs over, the one named last changes fastest.
Arguments:
- tensor: bfloat16 [1024, 1024, 1024], P('aa', 'ba', 'col'), may hold values from -6 to 6
- factor_two: bfloat16 [1024, 64], P('ba'), may hold values from -0.1875 to 0.1875
- factor_three: bfloat16 [1024, 64], P('col'), may hold values from -0.1875 to 0.1875
Outputs:
- gram: float32 [1024, 1024], P('aa', ('ba', 'col'))
The draws below stay inside these ranges and needn't reach their ends.
All inputs are finite; a program needn't handle non-finite values.
Results may differ from the reference program's by a relative error of at most 0.008.
Values sent between devices are 32-bit elements; how exact they have to be, the bound alone decides.
A program may use at most 64 MiB of HBM per device.

```python
import jax
import jax.numpy as jnp
from jax import lax

R = 64
C1 = 256
I1 = 1024
I2 = 1024
I3 = 1024


def steps_of(rng, dims, split, low, top_value):
    factor_of, own = 1.0, jax.random.fold_in(rng, 6)
    for axis_at, shards_of in split:
        heights = jnp.exp(jax.random.uniform(jax.random.fold_in(own, axis_at), (shards_of,), jnp.float32, low / len(split), top_value / len(split)))
        factor_of = factor_of * jnp.repeat(heights, dims[axis_at] // shards_of).reshape([-1 if axis == axis_at else 1 for axis in range(len(dims))])
    return factor_of


def bell_draw(stream_key, dims, spread, most, pieces=(), held_as=jnp.bfloat16):
    gain = steps_of(stream_key, dims, pieces, -0.22, 0.18) if pieces else 1.0
    entries = jax.random.normal(stream_key, dims, jnp.float32) * spread * gain
    return jnp.minimum(jnp.maximum(entries, -most), most).astype(held_as)


def setup_inputs(seed: int = 0) -> dict:
    key_list = jax.random.split(jax.random.key(seed), 4)
    tensor = bell_draw(key_list[0], (I1, I2, I3), 1.0, 6.0, ((0, 4), (1, 8), (2, 8)))
    factor_two = bell_draw(key_list[1], (I2, R), I2 ** -0.5, 0.1875, ((0, 8),))
    factor_three = bell_draw(key_list[2], (I3, R), I3 ** -0.5, 0.1875, ((0, 8),))
    return {"tensor": tensor, "factor_two": factor_two, "factor_three": factor_three}


def reference(tensor, factor_two, factor_three):
    second = factor_two.astype(jnp.float32)
    third = factor_three.astype(jnp.float32)
    blocks = tensor.reshape(I1 // C1, C1, I2, I3)

    def project(block):
        values = block.astype(jnp.float32)
        partial_value = jnp.einsum("ijk,ks->ijs", values, third, precision=lax.Precision.HIGHEST)
        partial_value = partial_value.astype(jnp.bfloat16).astype(jnp.float32)
        result = jnp.einsum("ijs,jr->irs", partial_value, second, precision=lax.Precision.HIGHEST)
        return result.reshape(C1, R * R)

    projected = lax.map(project, blocks).reshape(I1, R * R)
    gram = jnp.dot(projected, projected.T, precision=lax.Precision.HIGHEST, preferred_element_type=jnp.float32)
    return gram * (1.0 / (R * R))
```

```python
import jax
import jax.numpy as jnp
from jax import lax
from jax.sharding import PartitionSpec as P


def project(tensor, factor_two, factor_three):
    rank = factor_three.shape[1]
    local_rows = tensor.shape[0]
    local_two = tensor.shape[1]
    partial_value = jnp.einsum(
        "ijk,ks->jsi", tensor, factor_three, preferred_element_type=jnp.float32
    ).astype(jnp.bfloat16)
    flat_partial = partial_value.reshape(local_two, rank * local_rows)
    product = jnp.dot(factor_two.T, flat_partial, preferred_element_type=jnp.float32)
    return product.reshape(rank * rank, local_rows)


def a2a_rs(x, axis):
    n = lax.axis_size(axis)
    parts = x.reshape(n, x.shape[0] // n, *x.shape[1:])
    got = lax.all_to_all(parts, axis, 0, 0, tiled=False)
    return got.sum(axis=0)


def body(tensor, factor_two, factor_three):
    rank = factor_three.shape[1]
    product = project(tensor, factor_two, factor_three)
    columns_here = a2a_rs(a2a_rs(product, "col"), "ba")
    gathered = lax.all_gather(columns_here, "aa", axis=1, tiled=True)
    terms = jnp.dot(gathered.T, columns_here, precision=lax.Precision.HIGHEST, preferred_element_type=jnp.float32)
    gram_t = a2a_rs(a2a_rs(terms, "ba"), "col")
    return gram_t.T * (1.0 / (rank * rank))


def solution(mesh):
    return jax.shard_map(
        body,
        mesh=mesh,
        in_specs=(P("aa", "ba", "col"), P("ba", None), P("col", None)),
        out_specs=P("aa", ("ba", "col")),
        check_vma=False,
    )
```

```python
import functools

import jax
import jax.numpy as jnp
from jax import lax
from jax.experimental import pallas as pl
from jax.experimental.pallas import tpu as pltpu
from jax.sharding import PartitionSpec as P

MESH = pl.DeviceIdType.MESH


def ring_kernel(axis, n, x_ref, out_ref, recv, sendbuf, send_sem, recv_sem):
    me = lax.axis_index(axis)
    right = lax.rem(me + 1, n)
    left = lax.rem(me + n - 1, n)
    half = x_ref.shape[1] // 2
    lanes = (pl.ds(0, half), pl.ds(half, half))
    towards = (right, left)

    barrier = pltpu.get_barrier_semaphore()
    for neighbour in (left, right):
        pl.semaphore_signal(barrier, inc=1, device_id={axis: neighbour}, device_id_type=MESH)
    pl.semaphore_wait(barrier, 2)

    def chunk_sent(d, step):
        return lax.rem(me - step - 1 + 2 * n, n) if d == 0 else lax.rem(me + step + 1, n)

    for step in range(n - 1):
        copies = []
        for d in range(2):
            if step == 0:
                src = x_ref.at[chunk_sent(d, 0), lanes[d]]
            else:
                src = sendbuf.at[d, step]
            copy = pltpu.make_async_remote_copy(
                src_ref=src,
                dst_ref=recv.at[d, step],
                send_sem=send_sem.at[d, step],
                recv_sem=recv_sem.at[d, step],
                device_id={axis: towards[d]},
                device_id_type=MESH,
            )
            copy.start()
            copies.append(copy)
        for d in range(2):
            copies[d].wait_recv()
            got = chunk_sent(d, step + 1)
            total = recv[d, step] + x_ref[got, lanes[d]]
            if step < n - 2:
                sendbuf[d, step + 1] = total
            else:
                out_ref[lanes[d]] = total
        for d in range(2):
            copies[d].wait_send()


def ring_reduce_scatter(x, axis, n, collective_id):
    rows = x.shape[0] // n
    cols = x.shape[1]
    half = rows // 2
    parts = x.reshape(n, rows, cols)
    return pl.pallas_call(
        functools.partial(ring_kernel, axis, n),
        out_shape=jax.ShapeDtypeStruct((rows, cols), x.dtype),
        in_specs=[pl.BlockSpec(memory_space=pltpu.VMEM)],
        out_specs=pl.BlockSpec(memory_space=pltpu.VMEM),
        scratch_shapes=[
            pltpu.VMEM((2, n - 1, half, cols), x.dtype),
            pltpu.VMEM((2, n - 1, half, cols), x.dtype),
            pltpu.SemaphoreType.DMA((2, n - 1)),
            pltpu.SemaphoreType.DMA((2, n - 1)),
        ],
        compiler_params=pltpu.CompilerParams(collective_id=collective_id, has_side_effects=True),
    )(parts)


def project(tensor, factor_two, factor_three):
    rank = factor_three.shape[1]
    local_rows = tensor.shape[0]
    local_two = tensor.shape[1]
    partial_value = jnp.einsum(
        "ijk,ks->jsi", tensor, factor_three, preferred_element_type=jnp.float32
    ).astype(jnp.bfloat16)
    flat_partial = partial_value.reshape(local_two, rank * local_rows)
    product = jnp.dot(factor_two.T, flat_partial, preferred_element_type=jnp.float32)
    return product.reshape(rank * rank, local_rows)


def a2a_rs(x, axis):
    n = lax.axis_size(axis)
    parts = x.reshape(n, x.shape[0] // n, *x.shape[1:])
    got = lax.all_to_all(parts, axis, 0, 0, tiled=False)
    return got.sum(axis=0)


def body(tensor, factor_two, factor_three):
    rank = factor_three.shape[1]
    product = project(tensor, factor_two, factor_three)
    columns_here = a2a_rs(ring_reduce_scatter(product, "col", lax.axis_size("col"), 0), "ba")
    gathered = lax.all_gather(columns_here, "aa", axis=1, tiled=True)
    terms = jnp.dot(gathered.T, columns_here, precision=lax.Precision.HIGHEST, preferred_element_type=jnp.float32)
    gram_t = a2a_rs(a2a_rs(terms, "ba"), "col")
    return gram_t.T * (1.0 / (rank * rank))


def solution(mesh):
    return jax.shard_map(
        body,
        mesh=mesh,
        in_specs=(P("aa", "ba", "col"), P("ba", None), P("col", None)),
        out_specs=P("aa", ("ba", "col")),
        check_vma=False,
    )
```

```python
import functools

import jax
import jax.numpy as jnp
from jax import lax
from jax.experimental import pallas as pl
from jax.experimental.pallas import tpu as pltpu
from jax.sharding import PartitionSpec as P

MESH = pl.DeviceIdType.MESH


def ring_kernel(axis, n, x_ref, out_ref, recv, sendbuf, send_sem, recv_sem):
    me = lax.axis_index(axis)
    right = lax.rem(me + 1, n)
    left = lax.rem(me + n - 1, n)
    half = x_ref.shape[1] // 2
    lanes = (pl.ds(0, half), pl.ds(half, half))
    towards = (right, left)

    barrier = pltpu.get_barrier_semaphore()
    for neighbour in (left, right):
        pl.semaphore_signal(barrier, inc=1, device_id={axis: neighbour}, device_id_type=MESH)
    pl.semaphore_wait(barrier, 2)

    def chunk_sent(d, step):
        return lax.rem(me - step - 1 + 2 * n, n) if d == 0 else lax.rem(me + step + 1, n)

    for step in range(n - 1):
        copies = []
        for d in range(2):
            if step == 0:
                src = x_ref.at[chunk_sent(d, 0), lanes[d]]
            else:
                src = sendbuf.at[d, step]
            copy = pltpu.make_async_remote_copy(
                src_ref=src,
                dst_ref=recv.at[d, step],
                send_sem=send_sem.at[d, step],
                recv_sem=recv_sem.at[d, step],
                device_id={axis: towards[d]},
                device_id_type=MESH,
            )
            copy.start()
            copies.append(copy)
        for d in range(2):
            copies[d].wait_recv()
            got = chunk_sent(d, step + 1)
            total = recv[d, step] + x_ref[got, lanes[d]]
            if step < n - 2:
                sendbuf[d, step + 1] = total
            else:
                out_ref[lanes[d]] = total
        for d in range(2):
            copies[d].wait_send()


def ring_reduce_scatter(x, axis, n, collective_id):
    rows = x.shape[0] // n
    cols = x.shape[1]
    half = rows // 2
    parts = x.reshape(n, rows, cols)
    return pl.pallas_call(
        functools.partial(ring_kernel, axis, n),
        out_shape=jax.ShapeDtypeStruct((rows, cols), x.dtype),
        in_specs=[pl.BlockSpec(memory_space=pltpu.VMEM)],
        out_specs=pl.BlockSpec(memory_space=pltpu.VMEM),
        scratch_shapes=[
            pltpu.VMEM((2, n - 1, half, cols), x.dtype),
            pltpu.VMEM((2, n - 1, half, cols), x.dtype),
            pltpu.SemaphoreType.DMA((2, n - 1)),
            pltpu.SemaphoreType.DMA((2, n - 1)),
        ],
        compiler_params=pltpu.CompilerParams(collective_id=collective_id, has_side_effects=True),
    )(parts)


def group_index(axes, sizes):
    flat = lax.axis_index(axes[0])
    for axis, size in zip(axes[1:], sizes[1:]):
        flat = flat * size + lax.axis_index(axis)
    return flat


def group_device(axes, sizes, flat):
    place = {}
    for axis, size in reversed(list(zip(axes, sizes))):
        place[axis] = lax.rem(flat, size)
        flat = flat // size
    return place


def greet_all(axes, sizes, n, me):
    barrier = pltpu.get_barrier_semaphore()

    def greet(peer, carry):
        @pl.when(peer != me)
        def _():
            pl.semaphore_signal(barrier, inc=1, device_id=group_device(axes, sizes, peer), device_id_type=MESH)
        return carry

    lax.fori_loop(0, n, greet, 0)
    pl.semaphore_wait(barrier, n - 1)


def direct_rs_kernel(axes, sizes, x_ref, out_ref, recv, send_sem, recv_sem):
    n = x_ref.shape[0]
    me = group_index(axes, sizes)
    greet_all(axes, sizes, n, me)

    def outgoing(peer):
        return pltpu.make_async_remote_copy(
            src_ref=x_ref.at[peer],
            dst_ref=recv.at[me],
            send_sem=send_sem.at[peer],
            recv_sem=recv_sem.at[me],
            device_id=group_device(axes, sizes, peer),
            device_id_type=MESH,
        )

    def incoming(peer):
        return pltpu.make_async_remote_copy(
            src_ref=x_ref.at[me],
            dst_ref=recv.at[peer],
            send_sem=send_sem.at[peer],
            recv_sem=recv_sem.at[peer],
            device_id=group_device(axes, sizes, peer),
            device_id_type=MESH,
        )

    def start(step, carry):
        peer = lax.rem(me + step, n)
        outgoing(peer).start()
        return carry

    lax.fori_loop(1, n, start, 0)
    out_ref[...] = x_ref[me]

    def gather(step, carry):
        peer = lax.rem(me + n - step, n)
        incoming(peer).wait_recv()
        out_ref[...] += recv[peer]
        return carry

    lax.fori_loop(1, n, gather, 0)

    def finish(step, carry):
        peer = lax.rem(me + step, n)
        outgoing(peer).wait_send()
        return carry

    lax.fori_loop(1, n, finish, 0)


def direct_reduce_scatter(x, axes, sizes, collective_id):
    n = 1
    for size in sizes:
        n *= size
    rows = x.shape[0] // n
    cols = x.shape[1]
    parts = x.reshape(n, rows, cols)
    return pl.pallas_call(
        functools.partial(direct_rs_kernel, tuple(axes), tuple(sizes)),
        out_shape=jax.ShapeDtypeStruct((rows, cols), x.dtype),
        in_specs=[pl.BlockSpec(memory_space=pltpu.VMEM)],
        out_specs=pl.BlockSpec(memory_space=pltpu.VMEM),
        scratch_shapes=[
            pltpu.VMEM((n, rows, cols), x.dtype),
            pltpu.SemaphoreType.DMA((n,)),
            pltpu.SemaphoreType.DMA((n,)),
        ],
        compiler_params=pltpu.CompilerParams(collective_id=collective_id, has_side_effects=True),
    )(parts)


def direct_gather_kernel(axes, sizes, x_ref, out_ref, recv, send_sem, recv_sem):
    n = recv.shape[0]
    me = group_index(axes, sizes)
    greet_all(axes, sizes, n, me)

    def outgoing(peer):
        return pltpu.make_async_remote_copy(
            src_ref=x_ref,
            dst_ref=recv.at[me],
            send_sem=send_sem.at[peer],
            recv_sem=recv_sem.at[me],
            device_id=group_device(axes, sizes, peer),
            device_id_type=MESH,
        )

    def incoming(peer):
        return pltpu.make_async_remote_copy(
            src_ref=x_ref,
            dst_ref=recv.at[peer],
            send_sem=send_sem.at[peer],
            recv_sem=recv_sem.at[peer],
            device_id=group_device(axes, sizes, peer),
            device_id_type=MESH,
        )

    def start(step, carry):
        outgoing(lax.rem(me + step, n)).start()
        return carry

    lax.fori_loop(1, n, start, 0)
    out_ref[me] = x_ref[...]

    def gather(step, carry):
        peer = lax.rem(me + n - step, n)
        incoming(peer).wait_recv()
        out_ref[peer] = recv[peer]
        return carry

    lax.fori_loop(1, n, gather, 0)

    def finish(step, carry):
        outgoing(lax.rem(me + step, n)).wait_send()
        return carry

    lax.fori_loop(1, n, finish, 0)


def direct_all_gather(x, axes, sizes, collective_id):
    n = 1
    for size in sizes:
        n *= size
    return pl.pallas_call(
        functools.partial(direct_gather_kernel, tuple(axes), tuple(sizes)),
        out_shape=jax.ShapeDtypeStruct((n, *x.shape), x.dtype),
        in_specs=[pl.BlockSpec(memory_space=pltpu.VMEM)],
        out_specs=pl.BlockSpec(memory_space=pltpu.VMEM),
        scratch_shapes=[
            pltpu.VMEM((n, *x.shape), x.dtype),
            pltpu.SemaphoreType.DMA((n,)),
            pltpu.SemaphoreType.DMA((n,)),
        ],
        compiler_params=pltpu.CompilerParams(collective_id=collective_id, has_side_effects=True),
    )(x)


def project(tensor, factor_two, factor_three):
    rank = factor_three.shape[1]
    local_rows = tensor.shape[0]
    local_two = tensor.shape[1]
    partial_value = jnp.einsum(
        "ijk,ks->jsi", tensor, factor_three, preferred_element_type=jnp.float32
    ).astype(jnp.bfloat16)
    flat_partial = partial_value.reshape(local_two, rank * local_rows)
    product = jnp.dot(factor_two.T, flat_partial, preferred_element_type=jnp.float32)
    return product.reshape(rank * rank, local_rows)


def a2a_rs(x, axis):
    n = lax.axis_size(axis)
    parts = x.reshape(n, x.shape[0] // n, *x.shape[1:])
    got = lax.all_to_all(parts, axis, 0, 0, tiled=False)
    return got.sum(axis=0)


def body(tensor, factor_two, factor_three):
    rank = factor_three.shape[1]
    product = project(tensor, factor_two, factor_three)
    n_col, n_ba, n_aa = lax.axis_size("col"), lax.axis_size("ba"), lax.axis_size("aa")
    columns_here = direct_reduce_scatter(ring_reduce_scatter(product, "col", n_col, 0), ("ba",), (n_ba,), 3)
    gathered = direct_all_gather(columns_here, ("aa",), (n_aa,), 2)
    terms = jnp.einsum("pmj,mi->pji", gathered, columns_here, precision=lax.Precision.HIGHEST, preferred_element_type=jnp.float32)
    terms = terms.reshape(n_aa * columns_here.shape[1], columns_here.shape[1])
    gram_t = direct_reduce_scatter(terms, ("ba", "col"), (n_ba, n_col), 1)
    return gram_t.T * (1.0 / (rank * rank))


def solution(mesh):
    return jax.shard_map(
        body,
        mesh=mesh,
        in_specs=(P("aa", "ba", "col"), P("ba", None), P("col", None)),
        out_specs=P("aa", ("ba", "col")),
        check_vma=False,
    )
```

```python
import functools

import jax
import jax.numpy as jnp
from jax import lax
from jax.experimental import pallas as pl
from jax.experimental.pallas import tpu as pltpu
from jax.sharding import PartitionSpec as P

MESH = pl.DeviceIdType.MESH


def ring_kernel(axis, n, x_ref, out_ref, recv, sendbuf, send_sem, recv_sem):
    me = lax.axis_index(axis)
    right = lax.rem(me + 1, n)
    left = lax.rem(me + n - 1, n)
    half = x_ref.shape[1] // 2
    lanes = (pl.ds(0, half), pl.ds(half, half))
    towards = (right, left)

    barrier = pltpu.get_barrier_semaphore()
    for neighbour in (left, right):
        pl.semaphore_signal(barrier, inc=1, device_id={axis: neighbour}, device_id_type=MESH)
    pl.semaphore_wait(barrier, 2)

    def chunk_sent(d, step):
        return lax.rem(me - step - 1 + 2 * n, n) if d == 0 else lax.rem(me + step + 1, n)

    for step in range(n - 1):
        copies = []
        for d in range(2):
            if step == 0:
                src = x_ref.at[chunk_sent(d, 0), lanes[d]]
            else:
                src = sendbuf.at[d, step]
            copy = pltpu.make_async_remote_copy(
                src_ref=src,
                dst_ref=recv.at[d, step],
                send_sem=send_sem.at[d, step],
                recv_sem=recv_sem.at[d, step],
                device_id={axis: towards[d]},
                device_id_type=MESH,
            )
            copy.start()
            copies.append(copy)
        for d in range(2):
            copies[d].wait_recv()
            got = chunk_sent(d, step + 1)
            total = recv[d, step] + x_ref[got, lanes[d]]
            if step < n - 2:
                sendbuf[d, step + 1] = total
            else:
                out_ref[lanes[d]] = total
        for d in range(2):
            copies[d].wait_send()


def ring_reduce_scatter(x, axis, n, collective_id):
    rows = x.shape[0] // n
    cols = x.shape[1]
    half = rows // 2
    parts = x.reshape(n, rows, cols)
    return pl.pallas_call(
        functools.partial(ring_kernel, axis, n),
        out_shape=jax.ShapeDtypeStruct((rows, cols), x.dtype),
        in_specs=[pl.BlockSpec(memory_space=pltpu.VMEM)],
        out_specs=pl.BlockSpec(memory_space=pltpu.VMEM),
        scratch_shapes=[
            pltpu.VMEM((2, n - 1, half, cols), x.dtype),
            pltpu.VMEM((2, n - 1, half, cols), x.dtype),
            pltpu.SemaphoreType.DMA((2, n - 1)),
            pltpu.SemaphoreType.DMA((2, n - 1)),
        ],
        compiler_params=pltpu.CompilerParams(collective_id=collective_id, has_side_effects=True),
    )(parts)


def group_index(axes, sizes):
    flat = lax.axis_index(axes[0])
    for axis, size in zip(axes[1:], sizes[1:]):
        flat = flat * size + lax.axis_index(axis)
    return flat


def group_device(axes, sizes, flat):
    place = {}
    for axis, size in reversed(list(zip(axes, sizes))):
        place[axis] = lax.rem(flat, size)
        flat = flat // size
    return place


def greet_all(axes, sizes, n, me):
    barrier = pltpu.get_barrier_semaphore()

    def greet(peer, carry):
        @pl.when(peer != me)
        def _():
            pl.semaphore_signal(barrier, inc=1, device_id=group_device(axes, sizes, peer), device_id_type=MESH)
        return carry

    lax.fori_loop(0, n, greet, 0)
    pl.semaphore_wait(barrier, n - 1)


def direct_rs_kernel(axes, sizes, x_ref, out_ref, recv, send_sem, recv_sem):
    n = x_ref.shape[0]
    me = group_index(axes, sizes)
    greet_all(axes, sizes, n, me)

    def outgoing(peer):
        return pltpu.make_async_remote_copy(
            src_ref=x_ref.at[peer],
            dst_ref=recv.at[me],
            send_sem=send_sem.at[peer],
            recv_sem=recv_sem.at[me],
            device_id=group_device(axes, sizes, peer),
            device_id_type=MESH,
        )

    def incoming(peer):
        return pltpu.make_async_remote_copy(
            src_ref=x_ref.at[me],
            dst_ref=recv.at[peer],
            send_sem=send_sem.at[peer],
            recv_sem=recv_sem.at[peer],
            device_id=group_device(axes, sizes, peer),
            device_id_type=MESH,
        )

    def start(step, carry):
        peer = lax.rem(me + step, n)
        outgoing(peer).start()
        return carry

    lax.fori_loop(1, n, start, 0)
    out_ref[...] = x_ref[me]

    def gather(step, carry):
        peer = lax.rem(me + n - step, n)
        incoming(peer).wait_recv()
        out_ref[...] += recv[peer]
        return carry

    lax.fori_loop(1, n, gather, 0)

    def finish(step, carry):
        peer = lax.rem(me + step, n)
        outgoing(peer).wait_send()
        return carry

    lax.fori_loop(1, n, finish, 0)


def direct_reduce_scatter(x, axes, sizes, collective_id):
    n = 1
    for size in sizes:
        n *= size
    rows = x.shape[0] // n
    cols = x.shape[1]
    parts = x.reshape(n, rows, cols)
    return pl.pallas_call(
        functools.partial(direct_rs_kernel, tuple(axes), tuple(sizes)),
        out_shape=jax.ShapeDtypeStruct((rows, cols), x.dtype),
        in_specs=[pl.BlockSpec(memory_space=pltpu.VMEM)],
        out_specs=pl.BlockSpec(memory_space=pltpu.VMEM),
        scratch_shapes=[
            pltpu.VMEM((n, rows, cols), x.dtype),
            pltpu.SemaphoreType.DMA((n,)),
            pltpu.SemaphoreType.DMA((n,)),
        ],
        compiler_params=pltpu.CompilerParams(collective_id=collective_id, has_side_effects=True),
    )(parts)


def direct_gather_kernel(axes, sizes, x_ref, out_ref, recv, send_sem, recv_sem):
    n = recv.shape[0]
    me = group_index(axes, sizes)
    greet_all(axes, sizes, n, me)

    def outgoing(peer):
        return pltpu.make_async_remote_copy(
            src_ref=x_ref,
            dst_ref=recv.at[me],
            send_sem=send_sem.at[peer],
            recv_sem=recv_sem.at[me],
            device_id=group_device(axes, sizes, peer),
            device_id_type=MESH,
        )

    def incoming(peer):
        return pltpu.make_async_remote_copy(
            src_ref=x_ref,
            dst_ref=recv.at[peer],
            send_sem=send_sem.at[peer],
            recv_sem=recv_sem.at[peer],
            device_id=group_device(axes, sizes, peer),
            device_id_type=MESH,
        )

    def start(step, carry):
        outgoing(lax.rem(me + step, n)).start()
        return carry

    lax.fori_loop(1, n, start, 0)
    out_ref[me] = x_ref[...]

    def gather(step, carry):
        peer = lax.rem(me + n - step, n)
        incoming(peer).wait_recv()
        out_ref[peer] = recv[peer]
        return carry

    lax.fori_loop(1, n, gather, 0)

    def finish(step, carry):
        outgoing(lax.rem(me + step, n)).wait_send()
        return carry

    lax.fori_loop(1, n, finish, 0)


def direct_all_gather(x, axes, sizes, collective_id):
    n = 1
    for size in sizes:
        n *= size
    return pl.pallas_call(
        functools.partial(direct_gather_kernel, tuple(axes), tuple(sizes)),
        out_shape=jax.ShapeDtypeStruct((n, *x.shape), x.dtype),
        in_specs=[pl.BlockSpec(memory_space=pltpu.VMEM)],
        out_specs=pl.BlockSpec(memory_space=pltpu.VMEM),
        scratch_shapes=[
            pltpu.VMEM((n, *x.shape), x.dtype),
            pltpu.SemaphoreType.DMA((n,)),
            pltpu.SemaphoreType.DMA((n,)),
        ],
        compiler_params=pltpu.CompilerParams(collective_id=collective_id, has_side_effects=True),
    )(x)


def project(tensor, factor_two, factor_three):
    rank = factor_three.shape[1]
    local_rows = tensor.shape[0]
    local_two = tensor.shape[1]
    partial_value = jnp.einsum(
        "ijk,ks->jsi", tensor, factor_three, preferred_element_type=jnp.float32
    ).astype(jnp.bfloat16)
    flat_partial = partial_value.reshape(local_two, rank * local_rows)
    product = jnp.dot(factor_two.T, flat_partial, preferred_element_type=jnp.float32)
    return product.reshape(rank * rank, local_rows)


def body(tensor, factor_two, factor_three):
    rank = factor_three.shape[1]
    product = project(tensor, factor_two, factor_three)
    n_core, n_y, n_ba, n_aa = lax.axis_size("core"), lax.axis_size("y"), lax.axis_size("ba"), lax.axis_size("aa")
    n_col = n_core * n_y
    on_chip = direct_reduce_scatter(product, ("core",), (n_core,), 5)
    columns_here = direct_reduce_scatter(ring_reduce_scatter(on_chip, "y", n_y, 0), ("ba",), (n_ba,), 3)
    gathered = direct_all_gather(columns_here, ("aa",), (n_aa,), 2)
    depth, rows = columns_here.shape
    per_block = n_ba // n_aa
    out_rows = rows * n_aa // (n_ba * n_col)
    ordered = gathered.reshape(n_aa, depth, per_block, n_col, out_rows).transpose(3, 0, 2, 4, 1)
    terms = jnp.einsum("cpbtm,mi->cpbti", ordered, columns_here, precision=lax.Precision.HIGHEST, preferred_element_type=jnp.float32)
    terms = terms.reshape(n_col * n_ba * out_rows, rows)
    gram_t = direct_reduce_scatter(terms, ("y", "core"), (n_y, n_core), 1)
    gram_t = direct_reduce_scatter(gram_t, ("ba",), (n_ba,), 4)
    return gram_t.T * (1.0 / (rank * rank))


def solution(mesh):
    n_core = 2
    shape = mesh.devices.shape
    split = jax.sharding.Mesh(
        mesh.devices.reshape(shape[0], shape[1], shape[2] // n_core, n_core), ("aa", "ba", "y", "core")
    )
    return jax.shard_map(
        body,
        mesh=split,
        in_specs=(P("aa", "ba", ("y", "core")), P("ba", None), P(("y", "core"), None)),
        out_specs=P("aa", ("ba", "y", "core")),
        check_vma=False,
    )
```

```python
import functools

import jax
import jax.numpy as jnp
from jax import lax
from jax.experimental import pallas as pl
from jax.experimental.pallas import tpu as pltpu
from jax.sharding import PartitionSpec as P

MESH = pl.DeviceIdType.MESH


def ring_kernel(axis, n, x_ref, out_ref, recv, sendbuf, send_sem, recv_sem):
    me = lax.axis_index(axis)
    right = lax.rem(me + 1, n)
    left = lax.rem(me + n - 1, n)
    half = x_ref.shape[1] // 2
    lanes = (pl.ds(0, half), pl.ds(half, half))
    towards = (right, left)

    barrier = pltpu.get_barrier_semaphore()
    for neighbour in (left, right):
        pl.semaphore_signal(barrier, inc=1, device_id={axis: neighbour}, device_id_type=MESH)
    pl.semaphore_wait(barrier, 2)

    def chunk_sent(d, step):
        return lax.rem(me - step - 1 + 2 * n, n) if d == 0 else lax.rem(me + step + 1, n)

    for step in range(n - 1):
        copies = []
        for d in range(2):
            if step == 0:
                src = x_ref.at[chunk_sent(d, 0), lanes[d]]
            else:
                src = sendbuf.at[d, step]
            copy = pltpu.make_async_remote_copy(
                src_ref=src,
                dst_ref=recv.at[d, step],
                send_sem=send_sem.at[d, step],
                recv_sem=recv_sem.at[d, step],
                device_id={axis: towards[d]},
                device_id_type=MESH,
            )
            copy.start()
            copies.append(copy)
        for d in range(2):
            copies[d].wait_recv()
            got = chunk_sent(d, step + 1)
            total = recv[d, step] + x_ref[got, lanes[d]]
            if step < n - 2:
                sendbuf[d, step + 1] = total
            else:
                out_ref[lanes[d]] = total
        for d in range(2):
            copies[d].wait_send()


def ring_reduce_scatter(x, axis, n, collective_id):
    rows = x.shape[0] // n
    cols = x.shape[1]
    half = rows // 2
    parts = x.reshape(n, rows, cols)
    return pl.pallas_call(
        functools.partial(ring_kernel, axis, n),
        out_shape=jax.ShapeDtypeStruct((rows, cols), x.dtype),
        in_specs=[pl.BlockSpec(memory_space=pltpu.VMEM)],
        out_specs=pl.BlockSpec(memory_space=pltpu.VMEM),
        scratch_shapes=[
            pltpu.VMEM((2, n - 1, half, cols), x.dtype),
            pltpu.VMEM((2, n - 1, half, cols), x.dtype),
            pltpu.SemaphoreType.DMA((2, n - 1)),
            pltpu.SemaphoreType.DMA((2, n - 1)),
        ],
        compiler_params=pltpu.CompilerParams(collective_id=collective_id, has_side_effects=True),
    )(parts)


def group_index(axes, sizes):
    flat = lax.axis_index(axes[0])
    for axis, size in zip(axes[1:], sizes[1:]):
        flat = flat * size + lax.axis_index(axis)
    return flat


def group_device(axes, sizes, flat):
    place = {}
    for axis, size in reversed(list(zip(axes, sizes))):
        place[axis] = lax.rem(flat, size)
        flat = flat // size
    return place


def greet_all(axes, sizes, n, me):
    barrier = pltpu.get_barrier_semaphore()

    def greet(peer, carry):
        @pl.when(peer != me)
        def _():
            pl.semaphore_signal(barrier, inc=1, device_id=group_device(axes, sizes, peer), device_id_type=MESH)
        return carry

    lax.fori_loop(0, n, greet, 0)
    pl.semaphore_wait(barrier, n - 1)


def direct_rs_kernel(axes, sizes, x_ref, out_ref, recv, send_sem, recv_sem):
    n = x_ref.shape[0]
    me = group_index(axes, sizes)
    greet_all(axes, sizes, n, me)

    def outgoing(peer):
        return pltpu.make_async_remote_copy(
            src_ref=x_ref.at[peer],
            dst_ref=recv.at[me],
            send_sem=send_sem.at[peer],
            recv_sem=recv_sem.at[me],
            device_id=group_device(axes, sizes, peer),
            device_id_type=MESH,
        )

    def incoming(peer):
        return pltpu.make_async_remote_copy(
            src_ref=x_ref.at[me],
            dst_ref=recv.at[peer],
            send_sem=send_sem.at[peer],
            recv_sem=recv_sem.at[peer],
            device_id=group_device(axes, sizes, peer),
            device_id_type=MESH,
        )

    def start(step, carry):
        peer = lax.rem(me + step, n)
        outgoing(peer).start()
        return carry

    lax.fori_loop(1, n, start, 0)
    out_ref[...] = x_ref[me]

    def gather(step, carry):
        peer = lax.rem(me + n - step, n)
        incoming(peer).wait_recv()
        out_ref[...] += recv[peer]
        return carry

    lax.fori_loop(1, n, gather, 0)

    def finish(step, carry):
        peer = lax.rem(me + step, n)
        outgoing(peer).wait_send()
        return carry

    lax.fori_loop(1, n, finish, 0)


def direct_reduce_scatter(x, axes, sizes, collective_id):
    n = 1
    for size in sizes:
        n *= size
    rows = x.shape[0] // n
    cols = x.shape[1]
    parts = x.reshape(n, rows, cols)
    return pl.pallas_call(
        functools.partial(direct_rs_kernel, tuple(axes), tuple(sizes)),
        out_shape=jax.ShapeDtypeStruct((rows, cols), x.dtype),
        in_specs=[pl.BlockSpec(memory_space=pltpu.VMEM)],
        out_specs=pl.BlockSpec(memory_space=pltpu.VMEM),
        scratch_shapes=[
            pltpu.VMEM((n, rows, cols), x.dtype),
            pltpu.SemaphoreType.DMA((n,)),
            pltpu.SemaphoreType.DMA((n,)),
        ],
        compiler_params=pltpu.CompilerParams(collective_id=collective_id, has_side_effects=True),
    )(parts)


def direct_gather_kernel(axes, sizes, x_ref, out_ref, recv, send_sem, recv_sem):
    n = recv.shape[0]
    me = group_index(axes, sizes)
    greet_all(axes, sizes, n, me)

    def outgoing(peer):
        return pltpu.make_async_remote_copy(
            src_ref=x_ref,
            dst_ref=recv.at[me],
            send_sem=send_sem.at[peer],
            recv_sem=recv_sem.at[me],
            device_id=group_device(axes, sizes, peer),
            device_id_type=MESH,
        )

    def incoming(peer):
        return pltpu.make_async_remote_copy(
            src_ref=x_ref,
            dst_ref=recv.at[peer],
            send_sem=send_sem.at[peer],
            recv_sem=recv_sem.at[peer],
            device_id=group_device(axes, sizes, peer),
            device_id_type=MESH,
        )

    def start(step, carry):
        outgoing(lax.rem(me + step, n)).start()
        return carry

    lax.fori_loop(1, n, start, 0)
    out_ref[me] = x_ref[...]

    def gather(step, carry):
        peer = lax.rem(me + n - step, n)
        incoming(peer).wait_recv()
        out_ref[peer] = recv[peer]
        return carry

    lax.fori_loop(1, n, gather, 0)

    def finish(step, carry):
        outgoing(lax.rem(me + step, n)).wait_send()
        return carry

    lax.fori_loop(1, n, finish, 0)


def direct_all_gather(x, axes, sizes, collective_id):
    n = 1
    for size in sizes:
        n *= size
    return pl.pallas_call(
        functools.partial(direct_gather_kernel, tuple(axes), tuple(sizes)),
        out_shape=jax.ShapeDtypeStruct((n, *x.shape), x.dtype),
        in_specs=[pl.BlockSpec(memory_space=pltpu.VMEM)],
        out_specs=pl.BlockSpec(memory_space=pltpu.VMEM),
        scratch_shapes=[
            pltpu.VMEM((n, *x.shape), x.dtype),
            pltpu.SemaphoreType.DMA((n,)),
            pltpu.SemaphoreType.DMA((n,)),
        ],
        compiler_params=pltpu.CompilerParams(collective_id=collective_id, has_side_effects=True),
    )(x)


def project(tensor, factor_two, factor_three):
    rank = factor_three.shape[1]
    local_rows = tensor.shape[0]
    partial_value = jnp.einsum(
        "ijk,ks->ijs", tensor, factor_three, preferred_element_type=jnp.float32
    ).astype(jnp.bfloat16)
    product = jnp.einsum("jr,ijs->sri", factor_two, partial_value, preferred_element_type=jnp.float32)
    return product.reshape(rank * rank, local_rows)


def body(tensor, factor_two, factor_three):
    rank = factor_three.shape[1]
    product = project(tensor, factor_two, factor_three)
    n_core, n_y, n_ba, n_aa = lax.axis_size("core"), lax.axis_size("y"), lax.axis_size("ba"), lax.axis_size("aa")
    n_col = n_core * n_y
    on_chip = direct_reduce_scatter(product, ("core",), (n_core,), 5)
    columns_here = direct_reduce_scatter(ring_reduce_scatter(on_chip, "y", n_y, 0), ("ba",), (n_ba,), 3)
    gathered = direct_all_gather(columns_here, ("aa",), (n_aa,), 2)
    depth, rows = columns_here.shape
    per_block = n_ba // n_aa
    out_rows = rows * n_aa // (n_ba * n_col)
    ordered = gathered.reshape(n_aa, depth, per_block, n_col, out_rows).transpose(3, 0, 2, 4, 1)
    terms = jnp.einsum("cpbtm,mi->cpbti", ordered, columns_here, precision=lax.Precision.HIGHEST, preferred_element_type=jnp.float32)
    terms = terms.reshape(n_col * n_ba * out_rows, rows)
    gram_t = direct_reduce_scatter(terms, ("y", "core"), (n_y, n_core), 1)
    gram_t = direct_reduce_scatter(gram_t, ("ba",), (n_ba,), 4)
    return gram_t.T * (1.0 / (rank * rank))


def solution(mesh):
    n_core = 2
    shape = mesh.devices.shape
    split = jax.sharding.Mesh(
        mesh.devices.reshape(shape[0], shape[1], shape[2] // n_core, n_core), ("aa", "ba", "y", "core")
    )
    return jax.shard_map(
        body,
        mesh=split,
        in_specs=(P("aa", "ba", ("y", "core")), P("ba", None), P(("y", "core"), None)),
        out_specs=P("aa", ("ba", "y", "core")),
        check_vma=False,
    )
```

```python
import functools

import jax
import jax.numpy as jnp
from jax import lax
from jax.experimental import pallas as pl
from jax.experimental.pallas import tpu as pltpu
from jax.sharding import PartitionSpec as P

MESH = pl.DeviceIdType.MESH


def ring_kernel(axis, n, x_ref, out_ref, recv, sendbuf, send_sem, recv_sem):
    me = lax.axis_index(axis)
    right = lax.rem(me + 1, n)
    left = lax.rem(me + n - 1, n)
    half = x_ref.shape[1] // 2
    lanes = (pl.ds(0, half), pl.ds(half, half))
    towards = (right, left)

    barrier = pltpu.get_barrier_semaphore()
    for neighbour in (left, right):
        pl.semaphore_signal(barrier, inc=1, device_id={axis: neighbour}, device_id_type=MESH)
    pl.semaphore_wait(barrier, 2)

    def chunk_sent(d, step):
        return lax.rem(me - step - 1 + 2 * n, n) if d == 0 else lax.rem(me + step + 1, n)

    for step in range(n - 1):
        copies = []
        for d in range(2):
            if step == 0:
                src = x_ref.at[chunk_sent(d, 0), lanes[d]]
            else:
                src = sendbuf.at[d, step]
            copy = pltpu.make_async_remote_copy(
                src_ref=src,
                dst_ref=recv.at[d, step],
                send_sem=send_sem.at[d, step],
                recv_sem=recv_sem.at[d, step],
                device_id={axis: towards[d]},
                device_id_type=MESH,
            )
            copy.start()
            copies.append(copy)
        for d in range(2):
            copies[d].wait_recv()
            got = chunk_sent(d, step + 1)
            total = recv[d, step] + x_ref[got, lanes[d]]
            if step < n - 2:
                sendbuf[d, step + 1] = total
            else:
                out_ref[lanes[d]] = total
        for d in range(2):
            copies[d].wait_send()


def ring_reduce_scatter(x, axis, n, collective_id):
    rows = x.shape[0] // n
    cols = x.shape[1]
    half = rows // 2
    parts = x.reshape(n, rows, cols)
    return pl.pallas_call(
        functools.partial(ring_kernel, axis, n),
        out_shape=jax.ShapeDtypeStruct((rows, cols), x.dtype),
        in_specs=[pl.BlockSpec(memory_space=pltpu.VMEM)],
        out_specs=pl.BlockSpec(memory_space=pltpu.VMEM),
        scratch_shapes=[
            pltpu.VMEM((2, n - 1, half, cols), x.dtype),
            pltpu.VMEM((2, n - 1, half, cols), x.dtype),
            pltpu.SemaphoreType.DMA((2, n - 1)),
            pltpu.SemaphoreType.DMA((2, n - 1)),
        ],
        compiler_params=pltpu.CompilerParams(collective_id=collective_id, has_side_effects=True),
    )(parts)


def group_index(axes, sizes):
    flat = lax.axis_index(axes[0])
    for axis, size in zip(axes[1:], sizes[1:]):
        flat = flat * size + lax.axis_index(axis)
    return flat


def group_device(axes, sizes, flat):
    place = {}
    for axis, size in reversed(list(zip(axes, sizes))):
        place[axis] = lax.rem(flat, size)
        flat = flat // size
    return place


def greet_all(axes, sizes, n, me):
    barrier = pltpu.get_barrier_semaphore()

    def greet(peer, carry):
        @pl.when(peer != me)
        def _():
            pl.semaphore_signal(barrier, inc=1, device_id=group_device(axes, sizes, peer), device_id_type=MESH)
        return carry

    lax.fori_loop(0, n, greet, 0)
    pl.semaphore_wait(barrier, n - 1)


def direct_rs_kernel(axes, sizes, x_ref, out_ref, recv, send_sem, recv_sem):
    n = x_ref.shape[0]
    me = group_index(axes, sizes)
    greet_all(axes, sizes, n, me)

    def outgoing(peer):
        return pltpu.make_async_remote_copy(
            src_ref=x_ref.at[peer],
            dst_ref=recv.at[me],
            send_sem=send_sem.at[peer],
            recv_sem=recv_sem.at[me],
            device_id=group_device(axes, sizes, peer),
            device_id_type=MESH,
        )

    def incoming(peer):
        return pltpu.make_async_remote_copy(
            src_ref=x_ref.at[me],
            dst_ref=recv.at[peer],
            send_sem=send_sem.at[peer],
            recv_sem=recv_sem.at[peer],
            device_id=group_device(axes, sizes, peer),
            device_id_type=MESH,
        )

    def start(step, carry):
        peer = lax.rem(me + step, n)
        outgoing(peer).start()
        return carry

    lax.fori_loop(1, n, start, 0)
    out_ref[...] = x_ref[me]

    def gather(step, carry):
        peer = lax.rem(me + n - step, n)
        incoming(peer).wait_recv()
        out_ref[...] += recv[peer]
        return carry

    lax.fori_loop(1, n, gather, 0)

    def finish(step, carry):
        peer = lax.rem(me + step, n)
        outgoing(peer).wait_send()
        return carry

    lax.fori_loop(1, n, finish, 0)


def direct_reduce_scatter(x, axes, sizes, collective_id):
    n = 1
    for size in sizes:
        n *= size
    rows = x.shape[0] // n
    cols = x.shape[1]
    parts = x.reshape(n, rows, cols)
    return pl.pallas_call(
        functools.partial(direct_rs_kernel, tuple(axes), tuple(sizes)),
        out_shape=jax.ShapeDtypeStruct((rows, cols), x.dtype),
        in_specs=[pl.BlockSpec(memory_space=pltpu.VMEM)],
        out_specs=pl.BlockSpec(memory_space=pltpu.VMEM),
        scratch_shapes=[
            pltpu.VMEM((n, rows, cols), x.dtype),
            pltpu.SemaphoreType.DMA((n,)),
            pltpu.SemaphoreType.DMA((n,)),
        ],
        compiler_params=pltpu.CompilerParams(collective_id=collective_id, has_side_effects=True),
    )(parts)


def direct_gather_kernel(axes, sizes, x_ref, out_ref, recv, send_sem, recv_sem):
    n = recv.shape[0]
    me = group_index(axes, sizes)
    greet_all(axes, sizes, n, me)

    def outgoing(peer):
        return pltpu.make_async_remote_copy(
            src_ref=x_ref,
            dst_ref=recv.at[me],
            send_sem=send_sem.at[peer],
            recv_sem=recv_sem.at[me],
            device_id=group_device(axes, sizes, peer),
            device_id_type=MESH,
        )

    def incoming(peer):
        return pltpu.make_async_remote_copy(
            src_ref=x_ref,
            dst_ref=recv.at[peer],
            send_sem=send_sem.at[peer],
            recv_sem=recv_sem.at[peer],
            device_id=group_device(axes, sizes, peer),
            device_id_type=MESH,
        )

    def start(step, carry):
        outgoing(lax.rem(me + step, n)).start()
        return carry

    lax.fori_loop(1, n, start, 0)
    out_ref[me] = x_ref[...]

    def gather(step, carry):
        peer = lax.rem(me + n - step, n)
        incoming(peer).wait_recv()
        out_ref[peer] = recv[peer]
        return carry

    lax.fori_loop(1, n, gather, 0)

    def finish(step, carry):
        outgoing(lax.rem(me + step, n)).wait_send()
        return carry

    lax.fori_loop(1, n, finish, 0)


def direct_all_gather(x, axes, sizes, collective_id):
    n = 1
    for size in sizes:
        n *= size
    return pl.pallas_call(
        functools.partial(direct_gather_kernel, tuple(axes), tuple(sizes)),
        out_shape=jax.ShapeDtypeStruct((n, *x.shape), x.dtype),
        in_specs=[pl.BlockSpec(memory_space=pltpu.VMEM)],
        out_specs=pl.BlockSpec(memory_space=pltpu.VMEM),
        scratch_shapes=[
            pltpu.VMEM((n, *x.shape), x.dtype),
            pltpu.SemaphoreType.DMA((n,)),
            pltpu.SemaphoreType.DMA((n,)),
        ],
        compiler_params=pltpu.CompilerParams(collective_id=collective_id, has_side_effects=True),
    )(x)


def gram_kernel(sizes, q_ref, qt_ref, out_ref, gath, terms, recv_col, part, recv_ba, sems):
    n_aa, n_ba, n_y, n_core = sizes
    n_col = n_y * n_core
    per_block = n_ba // n_aa
    out_rows = out_ref.shape[0]
    send_g, recv_g, send_c, recv_c, send_b, recv_b = sems
    me_aa = lax.axis_index("aa")
    me_ba = lax.axis_index("ba")
    me_col = lax.axis_index("y") * n_core + lax.axis_index("core")

    def aa_dev(p):
        return {"aa": p}

    def col_dev(c):
        return {"y": c // n_core, "core": lax.rem(c, n_core)}

    def ba_dev(b):
        return {"ba": b}

    barrier = pltpu.get_barrier_semaphore()
    groups = ((n_aa, me_aa, aa_dev), (n_col, me_col, col_dev), (n_ba, me_ba, ba_dev))
    for n, me, dev in groups:
        def greet(step, carry, n=n, me=me, dev=dev):
            pl.semaphore_signal(barrier, inc=1, device_id=dev(lax.rem(me + step, n)), device_id_type=MESH)
            return carry

        lax.fori_loop(1, n, greet, 0)
    pl.semaphore_wait(barrier, n_aa + n_col + n_ba - 3)

    def copy(src, dst, send, recv, dev):
        return pltpu.make_async_remote_copy(
            src_ref=src, dst_ref=dst, send_sem=send, recv_sem=recv, device_id=dev, device_id_type=MESH
        )

    def g_out(p):
        return copy(qt_ref, gath.at[me_aa], send_g.at[p], recv_g.at[me_aa], aa_dev(p))

    def g_in(p):
        return copy(qt_ref, gath.at[p], send_g.at[p], recv_g.at[p], aa_dev(p))

    def g_start(step, carry):
        g_out(lax.rem(me_aa + step, n_aa)).start()
        return carry

    lax.fori_loop(1, n_aa, g_start, 0)
    gath[me_aa] = qt_ref[...]

    def g_wait(step, carry):
        g_in(lax.rem(me_aa + n_aa - step, n_aa)).wait_recv()
        return carry

    lax.fori_loop(1, n_aa, g_wait, 0)

    q = q_ref[...]
    for c in range(n_col):
        pieces = []
        for p in range(n_aa):
            for b2 in range(per_block):
                start = b2 * n_col * out_rows + c * out_rows
                pieces.append(gath[p, start:start + out_rows, :])
        lhs = jnp.concatenate(pieces, axis=0)
        block = jnp.dot(lhs, q, precision=lax.Precision.HIGHEST, preferred_element_type=jnp.float32)
        terms[c] = block.reshape(n_ba, out_rows, q.shape[1])

    def g_done(step, carry):
        g_out(lax.rem(me_aa + step, n_aa)).wait_send()
        return carry

    lax.fori_loop(1, n_aa, g_done, 0)

    def c_out(c):
        return copy(terms.at[c], recv_col.at[me_col], send_c.at[c], recv_c.at[me_col], col_dev(c))

    def c_in(c):
        return copy(terms.at[c], recv_col.at[c], send_c.at[c], recv_c.at[c], col_dev(c))

    def c_start(step, carry):
        c_out(lax.rem(me_col + step, n_col)).start()
        return carry

    lax.fori_loop(1, n_col, c_start, 0)
    part[...] = terms[me_col]

    def c_wait(step, carry):
        peer = lax.rem(me_col + n_col - step, n_col)
        c_in(peer).wait_recv()
        part[...] += recv_col[peer]
        return carry

    lax.fori_loop(1, n_col, c_wait, 0)

    def b_out(b):
        return copy(part.at[b], recv_ba.at[me_ba], send_b.at[b], recv_b.at[me_ba], ba_dev(b))

    def b_in(b):
        return copy(part.at[b], recv_ba.at[b], send_b.at[b], recv_b.at[b], ba_dev(b))

    def b_start(step, carry):
        b_out(lax.rem(me_ba + step, n_ba)).start()
        return carry

    lax.fori_loop(1, n_ba, b_start, 0)

    def c_done(step, carry):
        c_out(lax.rem(me_col + step, n_col)).wait_send()
        return carry

    lax.fori_loop(1, n_col, c_done, 0)
    out_ref[...] = part[me_ba]

    def b_wait(step, carry):
        peer = lax.rem(me_ba + n_ba - step, n_ba)
        b_in(peer).wait_recv()
        out_ref[...] += recv_ba[peer]
        return carry

    lax.fori_loop(1, n_ba, b_wait, 0)

    def b_done(step, carry):
        b_out(lax.rem(me_ba + step, n_ba)).wait_send()
        return carry

    lax.fori_loop(1, n_ba, b_done, 0)


def gram_reduce(q, sizes, collective_id):
    n_aa, n_ba, n_y, n_core = sizes
    n_col = n_y * n_core
    depth, rows = q.shape
    out_rows = rows * n_aa // (n_ba * n_col)
    f32 = jnp.float32
    return pl.pallas_call(
        functools.partial(gram_kernel, sizes),
        out_shape=jax.ShapeDtypeStruct((out_rows, rows), f32),
        in_specs=[pl.BlockSpec(memory_space=pltpu.VMEM)] * 2,
        out_specs=pl.BlockSpec(memory_space=pltpu.VMEM),
        scratch_shapes=[
            pltpu.VMEM((n_aa, rows, depth), f32),
            pltpu.VMEM((n_col, n_ba, out_rows, rows), f32),
            pltpu.VMEM((n_col, n_ba, out_rows, rows), f32),
            pltpu.VMEM((n_ba, out_rows, rows), f32),
            pltpu.VMEM((n_ba, out_rows, rows), f32),
            [pltpu.SemaphoreType.DMA((n_aa,)), pltpu.SemaphoreType.DMA((n_aa,)),
             pltpu.SemaphoreType.DMA((n_col,)), pltpu.SemaphoreType.DMA((n_col,)),
             pltpu.SemaphoreType.DMA((n_ba,)), pltpu.SemaphoreType.DMA((n_ba,))],
        ],
        compiler_params=pltpu.CompilerParams(collective_id=collective_id, has_side_effects=True),
    )(q, q.T)


def project(tensor, factor_two, factor_three):
    rank = factor_three.shape[1]
    local_rows = tensor.shape[0]
    partial_value = jnp.einsum(
        "ijk,ks->ijs", tensor, factor_three, preferred_element_type=jnp.float32
    ).astype(jnp.bfloat16)
    product = jnp.einsum("jr,ijs->sri", factor_two, partial_value, preferred_element_type=jnp.float32)
    return product.reshape(rank * rank, local_rows)


def body(tensor, factor_two, factor_three):
    rank = factor_three.shape[1]
    product = project(tensor, factor_two, factor_three)
    n_core, n_y, n_ba, n_aa = lax.axis_size("core"), lax.axis_size("y"), lax.axis_size("ba"), lax.axis_size("aa")
    on_chip = direct_reduce_scatter(product, ("core",), (n_core,), 5)
    columns_here = direct_reduce_scatter(ring_reduce_scatter(on_chip, "y", n_y, 0), ("ba",), (n_ba,), 3)
    gram_t = gram_reduce(columns_here, (n_aa, n_ba, n_y, n_core), 1)
    return gram_t.T * (1.0 / (rank * rank))
def solution(mesh):
    n_core = 2
    shape = mesh.devices.shape
    split = jax.sharding.Mesh(
        mesh.devices.reshape(shape[0], shape[1], shape[2] // n_core, n_core), ("aa", "ba", "y", "core")
    )
    return jax.shard_map(
        body,
        mesh=split,
        in_specs=(P("aa", "ba", ("y", "core")), P("ba", None), P(("y", "core"), None)),
        out_specs=P("aa", ("ba", "y", "core")),
        check_vma=False,
    )
```

```python
import functools

import jax
import jax.numpy as jnp
from jax import lax
from jax.experimental import pallas as pl
from jax.experimental.pallas import tpu as pltpu
from jax.sharding import PartitionSpec as P

MESH = pl.DeviceIdType.MESH


def remote(src, dst, send, recv, dev):
    return pltpu.make_async_remote_copy(
        src_ref=src, dst_ref=dst, send_sem=send, recv_sem=recv, device_id=dev, device_id_type=MESH
    )


def direct_phase(n, me, dev, x_ref, out_ref, recv, send_sem, recv_sem, blk=None):
    def piece(k):
        return x_ref.at[k] if blk is None else x_ref.at[pl.ds(k * blk, blk)]

    def outgoing(peer):
        return remote(piece(peer), recv.at[me], send_sem.at[peer], recv_sem.at[me], dev(peer))

    def incoming(peer):
        return remote(piece(me), recv.at[peer], send_sem.at[peer], recv_sem.at[peer], dev(peer))

    def start(step, carry):
        outgoing(lax.rem(me + step, n)).start()
        return carry

    lax.fori_loop(1, n, start, 0)
    out_ref[...] = piece(me)[...]

    def gather(step, carry):
        peer = lax.rem(me + n - step, n)
        incoming(peer).wait_recv()
        out_ref[...] += recv[peer]
        return carry

    lax.fori_loop(1, n, gather, 0)

    def finish(step, carry):
        outgoing(lax.rem(me + step, n)).wait_send()
        return carry

    lax.fori_loop(1, n, finish, 0)


def ring_phase(n, me, dev, x_ref, out_ref, recv, sendbuf, send_sem, recv_sem):
    right = lax.rem(me + 1, n)
    left = lax.rem(me + n - 1, n)
    half = x_ref.shape[1] // 2
    lanes = (pl.ds(0, half), pl.ds(half, half))
    towards = (right, left)

    def chunk_sent(d, step):
        return lax.rem(me - step - 1 + 2 * n, n) if d == 0 else lax.rem(me + step + 1, n)

    for step in range(n - 1):
        copies = []
        for d in range(2):
            src = x_ref.at[chunk_sent(d, 0), lanes[d]] if step == 0 else sendbuf.at[d, step]
            copy = remote(src, recv.at[d, step], send_sem.at[d, step], recv_sem.at[d, step], dev(towards[d]))
            copy.start()
            copies.append(copy)
        for d in range(2):
            copies[d].wait_recv()
            total = recv[d, step] + x_ref[chunk_sent(d, step + 1), lanes[d]]
            if step < n - 2:
                sendbuf[d, step + 1] = total
            else:
                out_ref[lanes[d]] = total
        for d in range(2):
            copies[d].wait_send()


def whole_kernel(sizes, x_ref, out_ref, core_recv, on_chip, ring_recv, ring_send, ring_out, ba_recv, q_buf,
                 gath, terms, recv_col, part, recv_ba, sems):
    n_aa, n_ba, n_y, n_core = sizes
    n_col = n_y * n_core
    per_block = n_ba // n_aa
    out_rows = out_ref.shape[0]
    (s_core, r_core, s_ring, r_ring, s_ba1, r_ba1, send_g, recv_g, send_c, recv_c, send_b, recv_b) = sems
    me_aa = lax.axis_index("aa")
    me_ba = lax.axis_index("ba")
    me_y = lax.axis_index("y")
    me_core = lax.axis_index("core")
    me_col = me_y * n_core + me_core

    def aa_dev(p):
        return {"aa": p}

    def col_dev(c):
        return {"y": c // n_core, "core": lax.rem(c, n_core)}

    def ba_dev(b):
        return {"ba": b}

    def core_dev(k):
        return {"core": k}

    def y_dev(k):
        return {"y": k}

    barrier = pltpu.get_barrier_semaphore()
    groups = ((n_aa, me_aa, aa_dev), (n_col, me_col, col_dev), (n_ba, me_ba, ba_dev))
    for n, me, dev in groups:
        def greet(step, carry, n=n, me=me, dev=dev):
            pl.semaphore_signal(barrier, inc=1, device_id=dev(lax.rem(me + step, n)), device_id_type=MESH)
            return carry

        lax.fori_loop(1, n, greet, 0)
    pl.semaphore_wait(barrier, n_aa + n_col + n_ba - 3)

    direct_phase(n_core, me_core, core_dev, x_ref, on_chip, core_recv, s_core, r_core)
    ring_phase(n_y, me_y, y_dev, on_chip, ring_out, ring_recv, ring_send, s_ring, r_ring)
    direct_phase(n_ba, me_ba, ba_dev, ring_out, q_buf, ba_recv, s_ba1, r_ba1, blk=q_buf.shape[0])

    q = q_buf[...]
    gath[me_aa] = q

    def g_out(p):
        return remote(q_buf, gath.at[me_aa], send_g.at[p], recv_g.at[me_aa], aa_dev(p))

    def g_in(p):
        return remote(q_buf, gath.at[p], send_g.at[p], recv_g.at[p], aa_dev(p))

    def g_start(step, carry):
        g_out(lax.rem(me_aa + step, n_aa)).start()
        return carry

    lax.fori_loop(1, n_aa, g_start, 0)

    def g_wait(step, carry):
        g_in(lax.rem(me_aa + n_aa - step, n_aa)).wait_recv()
        return carry

    lax.fori_loop(1, n_aa, g_wait, 0)

    def g_done(step, carry):
        g_out(lax.rem(me_aa + step, n_aa)).wait_send()
        return carry

    lax.fori_loop(1, n_aa, g_done, 0)

    blocks = [gath[p].T for p in range(n_aa)]
    for c in range(n_col):
        pieces = []
        for p in range(n_aa):
            for b2 in range(per_block):
                start = b2 * n_col * out_rows + c * out_rows
                pieces.append(blocks[p][start:start + out_rows, :])
        lhs = jnp.concatenate(pieces, axis=0)
        block = jnp.dot(lhs, q, precision=lax.Precision.HIGHEST, preferred_element_type=jnp.float32)
        terms[c] = block.reshape(n_ba, out_rows, q.shape[1])

    direct_phase(n_col, me_col, col_dev, terms, part, recv_col, send_c, recv_c)
    direct_phase(n_ba, me_ba, ba_dev, part, out_ref, recv_ba, send_b, recv_b)


def reduce_and_gram(product, sizes, collective_id):
    n_aa, n_ba, n_y, n_core = sizes
    n_col = n_y * n_core
    depth_all, rows = product.shape
    depth = depth_all // (n_core * n_y * n_ba)
    out_rows = rows * n_aa // (n_ba * n_col)
    rows_c = depth_all // n_core
    rows_y = rows_c // n_y
    half = rows_y // 2
    f32 = jnp.float32
    dma = pltpu.SemaphoreType.DMA
    return pl.pallas_call(
        functools.partial(whole_kernel, sizes),
        out_shape=jax.ShapeDtypeStruct((out_rows, rows), f32),
        in_specs=[pl.BlockSpec(memory_space=pltpu.VMEM)],
        out_specs=pl.BlockSpec(memory_space=pltpu.VMEM),
        scratch_shapes=[
            pltpu.VMEM((n_core, n_y, rows_y, rows), f32),
            pltpu.VMEM((n_y, rows_y, rows), f32),
            pltpu.VMEM((2, n_y - 1, half, rows), f32),
            pltpu.VMEM((2, n_y - 1, half, rows), f32),
            pltpu.VMEM((rows_y, rows), f32),
            pltpu.VMEM((n_ba, depth, rows), f32),
            pltpu.VMEM((depth, rows), f32),
            pltpu.VMEM((n_aa, depth, rows), f32),
            pltpu.VMEM((n_col, n_ba, out_rows, rows), f32),
            pltpu.VMEM((n_col, n_ba, out_rows, rows), f32),
            pltpu.VMEM((n_ba, out_rows, rows), f32),
            pltpu.VMEM((n_ba, out_rows, rows), f32),
            [dma((n_core,)), dma((n_core,)), dma((2, n_y - 1)), dma((2, n_y - 1)), dma((n_ba,)), dma((n_ba,)),
             dma((n_aa,)), dma((n_aa,)), dma((n_col,)), dma((n_col,)), dma((n_ba,)), dma((n_ba,))],
        ],
        compiler_params=pltpu.CompilerParams(collective_id=collective_id, has_side_effects=True),
    )(product.reshape(n_core, n_y, rows_y, rows))


def project(tensor, factor_two, factor_three):
    rank = factor_three.shape[1]
    local_rows = tensor.shape[0]
    partial_value = jnp.einsum(
        "ijk,ks->ijs", tensor, factor_three, preferred_element_type=jnp.float32
    ).astype(jnp.bfloat16)
    product = jnp.einsum("jr,ijs->sri", factor_two, partial_value, preferred_element_type=jnp.float32)
    return product.reshape(rank * rank, local_rows)


def body(tensor, factor_two, factor_three):
    rank = factor_three.shape[1]
    product = project(tensor, factor_two, factor_three)
    sizes = (lax.axis_size("aa"), lax.axis_size("ba"), lax.axis_size("y"), lax.axis_size("core"))
    gram_t = reduce_and_gram(product, sizes, 0)
    return gram_t.T * (1.0 / (rank * rank))
def solution(mesh):
    n_core = 2
    shape = mesh.devices.shape
    split = jax.sharding.Mesh(
        mesh.devices.reshape(shape[0], shape[1], shape[2] // n_core, n_core), ("aa", "ba", "y", "core")
    )
    return jax.shard_map(
        body,
        mesh=split,
        in_specs=(P("aa", "ba", ("y", "core")), P("ba", None), P(("y", "core"), None)),
        out_specs=P("aa", ("ba", "y", "core")),
        check_vma=False,
    )
```

```python
import functools

import jax
import jax.numpy as jnp
from jax import lax
from jax.experimental import pallas as pl
from jax.experimental.pallas import tpu as pltpu
from jax.sharding import PartitionSpec as P

MESH = pl.DeviceIdType.MESH


def remote(src, dst, send, recv, dev):
    return pltpu.make_async_remote_copy(
        src_ref=src, dst_ref=dst, send_sem=send, recv_sem=recv, device_id=dev, device_id_type=MESH
    )


def direct_phase(n, me, dev, x_ref, out_ref, recv, send_sem, recv_sem, blk=None):
    def piece(k):
        return x_ref.at[k] if blk is None else x_ref.at[pl.ds(k * blk, blk)]

    def outgoing(peer):
        return remote(piece(peer), recv.at[me], send_sem.at[peer], recv_sem.at[me], dev(peer))

    def incoming(peer):
        return remote(piece(me), recv.at[peer], send_sem.at[peer], recv_sem.at[peer], dev(peer))

    def start(step, carry):
        outgoing(lax.rem(me + step, n)).start()
        return carry

    lax.fori_loop(1, n, start, 0)
    out_ref[...] = piece(me)[...]

    def gather(step, carry):
        peer = lax.rem(me + n - step, n)
        incoming(peer).wait_recv()
        out_ref[...] += recv[peer]
        return carry

    lax.fori_loop(1, n, gather, 0)

    def finish(step, carry):
        outgoing(lax.rem(me + step, n)).wait_send()
        return carry

    lax.fori_loop(1, n, finish, 0)


def direct_start(n, me, dev, x_ref, recv, send_sem, recv_sem, blk):
    def start(step, carry):
        peer = lax.rem(me + step, n)
        remote(x_ref.at[pl.ds(peer * blk, blk)], recv.at[me], send_sem.at[peer], recv_sem.at[me], dev(peer)).start()
        return carry

    lax.fori_loop(1, n, start, 0)


def direct_finish(n, me, dev, x_ref, out_ref, recv, send_sem, recv_sem, blk):
    out_ref[...] = x_ref[pl.ds(me * blk, blk)]

    def gather(step, carry):
        peer = lax.rem(me + n - step, n)
        remote(x_ref.at[pl.ds(me * blk, blk)], recv.at[peer], send_sem.at[peer], recv_sem.at[peer], dev(peer)).wait_recv()
        out_ref[...] += recv[peer]
        return carry

    lax.fori_loop(1, n, gather, 0)

    def finish(step, carry):
        peer = lax.rem(me + step, n)
        remote(x_ref.at[pl.ds(peer * blk, blk)], recv.at[me], send_sem.at[peer], recv_sem.at[me], dev(peer)).wait_send()
        return carry

    lax.fori_loop(1, n, finish, 0)


def ring_flat(n, me, dev, x_ref, out_ref, recv, sendbuf, send_sem, recv_sem, blk):
    right = lax.rem(me + 1, n)
    left = lax.rem(me + n - 1, n)
    half = blk // 2
    towards = (right, left)

    def chunk_sent(d, step):
        return lax.rem(me - step - 1 + 2 * n, n) if d == 0 else lax.rem(me + step + 1, n)

    def rows_of(d, chunk):
        return pl.ds(chunk * blk + d * half, half)

    for step in range(n - 1):
        copies = []
        for d in range(2):
            src = x_ref.at[rows_of(d, chunk_sent(d, 0))] if step == 0 else sendbuf.at[d, step]
            copy = remote(src, recv.at[d, step], send_sem.at[d, step], recv_sem.at[d, step], dev(towards[d]))
            copy.start()
            copies.append(copy)
        for d in range(2):
            copies[d].wait_recv()
            total = recv[d, step] + x_ref[rows_of(d, chunk_sent(d, step + 1))]
            if step < n - 2:
                sendbuf[d, step + 1] = total
            else:
                out_ref[pl.ds(d * half, half)] = total
        for d in range(2):
            copies[d].wait_send()


def ring_phase(n, me, dev, x_ref, out_ref, recv, sendbuf, send_sem, recv_sem):
    right = lax.rem(me + 1, n)
    left = lax.rem(me + n - 1, n)
    half = x_ref.shape[1] // 2
    lanes = (pl.ds(0, half), pl.ds(half, half))
    towards = (right, left)

    def chunk_sent(d, step):
        return lax.rem(me - step - 1 + 2 * n, n) if d == 0 else lax.rem(me + step + 1, n)

    for step in range(n - 1):
        copies = []
        for d in range(2):
            src = x_ref.at[chunk_sent(d, 0), lanes[d]] if step == 0 else sendbuf.at[d, step]
            copy = remote(src, recv.at[d, step], send_sem.at[d, step], recv_sem.at[d, step], dev(towards[d]))
            copy.start()
            copies.append(copy)
        for d in range(2):
            copies[d].wait_recv()
            total = recv[d, step] + x_ref[chunk_sent(d, step + 1), lanes[d]]
            if step < n - 2:
                sendbuf[d, step + 1] = total
            else:
                out_ref[lanes[d]] = total
        for d in range(2):
            copies[d].wait_send()


def whole_kernel(sizes, x_ref, out_ref, core_recv, on_chip, ring_a_recv, ring_a_send, ring_a_out, z_b_recv, z_b_out,
                 z_a_recv, ring_b_recv, ring_b_send, q_buf, gath, terms, recv_col, part, recv_ba, sems):
    n_aa, n_ba, n_y, n_core = sizes
    n_col = n_y * n_core
    per_block = n_ba // n_aa
    out_rows = out_ref.shape[0]
    (s_core, r_core, s_ra, r_ra, s_zb, r_zb, s_za, r_za, s_rb, r_rb, send_g, recv_g, send_c, recv_c, send_b, recv_b) = sems
    me_aa = lax.axis_index("aa")
    me_ba = lax.axis_index("ba")
    me_y = lax.axis_index("y")
    me_core = lax.axis_index("core")
    me_col = me_y * n_core + me_core

    def aa_dev(p):
        return {"aa": p}

    def col_dev(c):
        return {"y": c // n_core, "core": lax.rem(c, n_core)}

    def ba_dev(b):
        return {"ba": b}

    def core_dev(k):
        return {"core": k}

    def y_dev(k):
        return {"y": k}

    barrier = pltpu.get_barrier_semaphore()
    groups = ((n_aa, me_aa, aa_dev), (n_col, me_col, col_dev), (n_ba, me_ba, ba_dev))
    for n, me, dev in groups:
        def greet(step, carry, n=n, me=me, dev=dev):
            pl.semaphore_signal(barrier, inc=1, device_id=dev(lax.rem(me + step, n)), device_id_type=MESH)
            return carry

        lax.fori_loop(1, n, greet, 0)
    pl.semaphore_wait(barrier, n_aa + n_col + n_ba - 3)

    direct_phase(n_core, me_core, core_dev, x_ref, on_chip, core_recv, s_core, r_core)
    rows_a = on_chip.shape[0] * 3 // 4
    rows_b = on_chip.shape[0] - rows_a
    part_a = on_chip.at[pl.ds(0, rows_a)]
    part_b = on_chip.at[pl.ds(rows_a, rows_b)]
    blk_zb = rows_b // n_ba
    direct_start(n_ba, me_ba, ba_dev, part_b, z_b_recv, s_zb, r_zb, blk_zb)
    ring_flat(n_y, me_y, y_dev, part_a, ring_a_out, ring_a_recv, ring_a_send, s_ra, r_ra, rows_a // n_y)
    direct_finish(n_ba, me_ba, ba_dev, part_b, z_b_out, z_b_recv, s_zb, r_zb, blk_zb)
    depth_a = ring_a_out.shape[0] // n_ba
    depth_b = blk_zb // n_y
    direct_start(n_ba, me_ba, ba_dev, ring_a_out, z_a_recv, s_za, r_za, depth_a)
    ring_flat(n_y, me_y, y_dev, z_b_out, q_buf.at[pl.ds(depth_a, depth_b)], ring_b_recv, ring_b_send, s_rb, r_rb, depth_b)
    direct_finish(n_ba, me_ba, ba_dev, ring_a_out, q_buf.at[pl.ds(0, depth_a)], z_a_recv, s_za, r_za, depth_a)

    q = q_buf[...]
    gath[me_aa] = q

    def g_out(p):
        return remote(q_buf, gath.at[me_aa], send_g.at[p], recv_g.at[me_aa], aa_dev(p))

    def g_in(p):
        return remote(q_buf, gath.at[p], send_g.at[p], recv_g.at[p], aa_dev(p))

    def g_start(step, carry):
        g_out(lax.rem(me_aa + step, n_aa)).start()
        return carry

    lax.fori_loop(1, n_aa, g_start, 0)

    def g_wait(step, carry):
        g_in(lax.rem(me_aa + n_aa - step, n_aa)).wait_recv()
        return carry

    lax.fori_loop(1, n_aa, g_wait, 0)

    def g_done(step, carry):
        g_out(lax.rem(me_aa + step, n_aa)).wait_send()
        return carry

    lax.fori_loop(1, n_aa, g_done, 0)

    blocks = [gath[p].T for p in range(n_aa)]
    for c in range(n_col):
        pieces = []
        for p in range(n_aa):
            for b2 in range(per_block):
                start = b2 * n_col * out_rows + c * out_rows
                pieces.append(blocks[p][start:start + out_rows, :])
        lhs = jnp.concatenate(pieces, axis=0)
        block = jnp.dot(lhs, q, precision=lax.Precision.HIGHEST, preferred_element_type=jnp.float32)
        terms[c] = block.reshape(n_ba, out_rows, q.shape[1])

    direct_phase(n_col, me_col, col_dev, terms, part, recv_col, send_c, recv_c)
    direct_phase(n_ba, me_ba, ba_dev, part, out_ref, recv_ba, send_b, recv_b)


def reduce_and_gram(product, sizes, collective_id):
    n_aa, n_ba, n_y, n_core = sizes
    n_col = n_y * n_core
    depth_all, rows = product.shape
    depth = depth_all // (n_core * n_y * n_ba)
    out_rows = rows * n_aa // (n_ba * n_col)
    rows_c = depth_all // n_core
    rows_a = rows_c * 3 // 4
    blk_a = rows_a // n_y
    blk_zb = (rows_c - rows_a) // n_ba
    depth_a = blk_a // n_ba
    depth_b = blk_zb // n_y
    f32 = jnp.float32
    dma = pltpu.SemaphoreType.DMA
    return pl.pallas_call(
        functools.partial(whole_kernel, sizes),
        out_shape=jax.ShapeDtypeStruct((out_rows, rows), f32),
        in_specs=[pl.BlockSpec(memory_space=pltpu.VMEM)],
        out_specs=pl.BlockSpec(memory_space=pltpu.VMEM),
        scratch_shapes=[
            pltpu.VMEM((n_core, rows_c, rows), f32),
            pltpu.VMEM((rows_c, rows), f32),
            pltpu.VMEM((2, n_y - 1, blk_a // 2, rows), f32),
            pltpu.VMEM((2, n_y - 1, blk_a // 2, rows), f32),
            pltpu.VMEM((blk_a, rows), f32),
            pltpu.VMEM((n_ba, blk_zb, rows), f32),
            pltpu.VMEM((blk_zb, rows), f32),
            pltpu.VMEM((n_ba, depth_a, rows), f32),
            pltpu.VMEM((2, n_y - 1, depth_b // 2, rows), f32),
            pltpu.VMEM((2, n_y - 1, depth_b // 2, rows), f32),
            pltpu.VMEM((depth, rows), f32),
            pltpu.VMEM((n_aa, depth, rows), f32),
            pltpu.VMEM((n_col, n_ba, out_rows, rows), f32),
            pltpu.VMEM((n_col, n_ba, out_rows, rows), f32),
            pltpu.VMEM((n_ba, out_rows, rows), f32),
            pltpu.VMEM((n_ba, out_rows, rows), f32),
            [dma((n_core,)), dma((n_core,)), dma((2, n_y - 1)), dma((2, n_y - 1)), dma((n_ba,)), dma((n_ba,)),
             dma((n_ba,)), dma((n_ba,)), dma((2, n_y - 1)), dma((2, n_y - 1)),
             dma((n_aa,)), dma((n_aa,)), dma((n_col,)), dma((n_col,)), dma((n_ba,)), dma((n_ba,))],
        ],
        compiler_params=pltpu.CompilerParams(collective_id=collective_id, has_side_effects=True),
    )(product.reshape(n_core, rows_c, rows))


def project(tensor, factor_two, factor_three):
    rank = factor_three.shape[1]
    local_rows = tensor.shape[0]
    partial_value = jnp.einsum(
        "ijk,ks->ijs", tensor, factor_three, preferred_element_type=jnp.float32
    ).astype(jnp.bfloat16)
    product = jnp.einsum("jr,ijs->sri", factor_two, partial_value, preferred_element_type=jnp.float32)
    return product.reshape(rank * rank, local_rows)


def body(tensor, factor_two, factor_three):
    rank = factor_three.shape[1]
    product = project(tensor, factor_two, factor_three)
    sizes = (lax.axis_size("aa"), lax.axis_size("ba"), lax.axis_size("y"), lax.axis_size("core"))
    gram_t = reduce_and_gram(product, sizes, 0)
    return gram_t.T * (1.0 / (rank * rank))
def solution(mesh):
    n_core = 2
    shape = mesh.devices.shape
    split = jax.sharding.Mesh(
        mesh.devices.reshape(shape[0], shape[1], shape[2] // n_core, n_core), ("aa", "ba", "y", "core")
    )
    return jax.shard_map(
        body,
        mesh=split,
        in_specs=(P("aa", "ba", ("y", "core")), P("ba", None), P(("y", "core"), None)),
        out_specs=P("aa", ("ba", "y", "core")),
        check_vma=False,
    )
```

```python
import functools

import jax
import jax.numpy as jnp
from jax import lax
from jax.experimental import pallas as pl
from jax.experimental.pallas import tpu as pltpu
from jax.sharding import PartitionSpec as P

MESH = pl.DeviceIdType.MESH


def remote(src, dst, send, recv, dev):
    return pltpu.make_async_remote_copy(
        src_ref=src, dst_ref=dst, send_sem=send, recv_sem=recv, device_id=dev, device_id_type=MESH
    )


def direct_phase(n, me, dev, x_ref, out_ref, recv, send_sem, recv_sem, blk=None):
    def piece(k):
        return x_ref.at[k] if blk is None else x_ref.at[pl.ds(k * blk, blk)]

    def outgoing(peer):
        return remote(piece(peer), recv.at[me], send_sem.at[peer], recv_sem.at[me], dev(peer))

    def incoming(peer):
        return remote(piece(me), recv.at[peer], send_sem.at[peer], recv_sem.at[peer], dev(peer))

    def start(step, carry):
        outgoing(lax.rem(me + step, n)).start()
        return carry

    lax.fori_loop(1, n, start, 0)
    out_ref[...] = piece(me)[...]

    def gather(step, carry):
        peer = lax.rem(me + n - step, n)
        incoming(peer).wait_recv()
        out_ref[...] += recv[peer]
        return carry

    lax.fori_loop(1, n, gather, 0)

    def finish(step, carry):
        outgoing(lax.rem(me + step, n)).wait_send()
        return carry

    lax.fori_loop(1, n, finish, 0)


def direct_start(n, me, dev, x_ref, recv, send_sem, recv_sem, blk):
    def start(step, carry):
        peer = lax.rem(me + step, n)
        remote(x_ref.at[pl.ds(peer * blk, blk)], recv.at[me], send_sem.at[peer], recv_sem.at[me], dev(peer)).start()
        return carry

    lax.fori_loop(1, n, start, 0)


def direct_finish(n, me, dev, x_ref, out_ref, recv, send_sem, recv_sem, blk):
    out_ref[...] = x_ref[pl.ds(me * blk, blk)]

    def gather(step, carry):
        peer = lax.rem(me + n - step, n)
        remote(x_ref.at[pl.ds(me * blk, blk)], recv.at[peer], send_sem.at[peer], recv_sem.at[peer], dev(peer)).wait_recv()
        out_ref[...] += recv[peer]
        return carry

    lax.fori_loop(1, n, gather, 0)

    def finish(step, carry):
        peer = lax.rem(me + step, n)
        remote(x_ref.at[pl.ds(peer * blk, blk)], recv.at[me], send_sem.at[peer], recv_sem.at[me], dev(peer)).wait_send()
        return carry

    lax.fori_loop(1, n, finish, 0)


def ring_flat(n, me, dev, x_ref, out_ref, recv, sendbuf, send_sem, recv_sem, blk):
    right = lax.rem(me + 1, n)
    left = lax.rem(me + n - 1, n)
    half = blk // 2
    towards = (right, left)

    def chunk_sent(d, step):
        return lax.rem(me - step - 1 + 2 * n, n) if d == 0 else lax.rem(me + step + 1, n)

    def rows_of(d, chunk):
        return pl.ds(chunk * blk + d * half, half)

    for step in range(n - 1):
        copies = []
        for d in range(2):
            src = x_ref.at[rows_of(d, chunk_sent(d, 0))] if step == 0 else sendbuf.at[d, step]
            copy = remote(src, recv.at[d, step], send_sem.at[d, step], recv_sem.at[d, step], dev(towards[d]))
            copy.start()
            copies.append(copy)
        for d in range(2):
            copies[d].wait_recv()
            total = recv[d, step] + x_ref[rows_of(d, chunk_sent(d, step + 1))]
            if step < n - 2:
                sendbuf[d, step + 1] = total
            else:
                out_ref[pl.ds(d * half, half)] = total
        for d in range(2):
            copies[d].wait_send()


def ring_phase(n, me, dev, x_ref, out_ref, recv, sendbuf, send_sem, recv_sem):
    right = lax.rem(me + 1, n)
    left = lax.rem(me + n - 1, n)
    half = x_ref.shape[1] // 2
    lanes = (pl.ds(0, half), pl.ds(half, half))
    towards = (right, left)

    def chunk_sent(d, step):
        return lax.rem(me - step - 1 + 2 * n, n) if d == 0 else lax.rem(me + step + 1, n)

    for step in range(n - 1):
        copies = []
        for d in range(2):
            src = x_ref.at[chunk_sent(d, 0), lanes[d]] if step == 0 else sendbuf.at[d, step]
            copy = remote(src, recv.at[d, step], send_sem.at[d, step], recv_sem.at[d, step], dev(towards[d]))
            copy.start()
            copies.append(copy)
        for d in range(2):
            copies[d].wait_recv()
            total = recv[d, step] + x_ref[chunk_sent(d, step + 1), lanes[d]]
            if step < n - 2:
                sendbuf[d, step + 1] = total
            else:
                out_ref[lanes[d]] = total
        for d in range(2):
            copies[d].wait_send()


def whole_kernel(sizes, x_ref, out_ref, core_recv, on_chip, ring_a_recv, ring_a_send, ring_a_out, z_b_recv, z_b_out,
                 z_a_recv, ring_b_recv, ring_b_send, q_buf, gath, gt, terms, recv_col, part, recv_ba, sems):
    n_aa, n_ba, n_y, n_core = sizes
    n_col = n_y * n_core
    per_block = n_ba // n_aa
    out_rows = out_ref.shape[0]
    (s_core, r_core, s_ra, r_ra, s_zb, r_zb, s_za, r_za, s_rb, r_rb, send_g, recv_g, send_c, recv_c, send_b, recv_b) = sems
    me_aa = lax.axis_index("aa")
    me_ba = lax.axis_index("ba")
    me_y = lax.axis_index("y")
    me_core = lax.axis_index("core")
    me_col = me_y * n_core + me_core

    def aa_dev(p):
        return {"aa": p}

    def col_dev(c):
        return {"y": c // n_core, "core": lax.rem(c, n_core)}

    def ba_dev(b):
        return {"ba": b}

    def core_dev(k):
        return {"core": k}

    def y_dev(k):
        return {"y": k}

    barrier = pltpu.get_barrier_semaphore()
    groups = ((n_aa, me_aa, aa_dev), (n_col, me_col, col_dev), (n_ba, me_ba, ba_dev))
    for n, me, dev in groups:
        def greet(step, carry, n=n, me=me, dev=dev):
            pl.semaphore_signal(barrier, inc=1, device_id=dev(lax.rem(me + step, n)), device_id_type=MESH)
            return carry

        lax.fori_loop(1, n, greet, 0)
    pl.semaphore_wait(barrier, n_aa + n_col + n_ba - 3)

    direct_phase(n_core, me_core, core_dev, x_ref, on_chip, core_recv, s_core, r_core)
    rows_a = on_chip.shape[0] * 3 // 4
    rows_b = on_chip.shape[0] - rows_a
    part_a = on_chip.at[pl.ds(0, rows_a)]
    part_b = on_chip.at[pl.ds(rows_a, rows_b)]
    blk_zb = rows_b // n_ba
    direct_start(n_ba, me_ba, ba_dev, part_b, z_b_recv, s_zb, r_zb, blk_zb)
    ring_flat(n_y, me_y, y_dev, part_a, ring_a_out, ring_a_recv, ring_a_send, s_ra, r_ra, rows_a // n_y)
    direct_finish(n_ba, me_ba, ba_dev, part_b, z_b_out, z_b_recv, s_zb, r_zb, blk_zb)
    depth_a = ring_a_out.shape[0] // n_ba
    depth_b = blk_zb // n_y
    direct_start(n_ba, me_ba, ba_dev, ring_a_out, z_a_recv, s_za, r_za, depth_a)
    ring_flat(n_y, me_y, y_dev, z_b_out, q_buf.at[pl.ds(depth_a, depth_b)], ring_b_recv, ring_b_send, s_rb, r_rb, depth_b)
    direct_finish(n_ba, me_ba, ba_dev, ring_a_out, q_buf.at[pl.ds(0, depth_a)], z_a_recv, s_za, r_za, depth_a)

    q = q_buf[...]
    gath[me_aa] = q

    def g_out(p):
        return remote(q_buf, gath.at[me_aa], send_g.at[p], recv_g.at[me_aa], aa_dev(p))

    def g_in(p):
        return remote(q_buf, gath.at[p], send_g.at[p], recv_g.at[p], aa_dev(p))

    def g_start(step, carry):
        g_out(lax.rem(me_aa + step, n_aa)).start()
        return carry

    lax.fori_loop(1, n_aa, g_start, 0)

    def g_wait(step, carry):
        g_in(lax.rem(me_aa + n_aa - step, n_aa)).wait_recv()
        return carry

    lax.fori_loop(1, n_aa, g_wait, 0)

    def g_done(step, carry):
        g_out(lax.rem(me_aa + step, n_aa)).wait_send()
        return carry

    lax.fori_loop(1, n_aa, g_done, 0)

    for p in range(n_aa):
        gt[p] = gath[p].T

    def term_block(c):
        pieces = []
        for p in range(n_aa):
            for b2 in range(per_block):
                start = pl.multiple_of(b2 * n_col * out_rows + c * out_rows, out_rows)
                pieces.append(gt[p, pl.ds(start, out_rows), :])
        lhs = jnp.concatenate(pieces, axis=0)
        block = jnp.dot(lhs, q, precision=lax.Precision.HIGHEST, preferred_element_type=jnp.float32)
        return block.reshape(n_ba, out_rows, q.shape[1])

    def c_out(c):
        return remote(terms.at[c], recv_col.at[me_col], send_c.at[c], recv_c.at[me_col], col_dev(c))

    def c_in(c):
        return remote(terms.at[me_col], recv_col.at[c], send_c.at[c], recv_c.at[c], col_dev(c))

    def c_start(step, carry):
        c = lax.rem(me_col + step, n_col)
        terms[c] = term_block(c)
        c_out(c).start()
        return carry

    lax.fori_loop(1, n_col, c_start, 0)
    part[...] = term_block(me_col)

    def c_wait(step, carry):
        peer = lax.rem(me_col + n_col - step, n_col)
        c_in(peer).wait_recv()
        part[...] += recv_col[peer]
        return carry

    lax.fori_loop(1, n_col, c_wait, 0)

    def c_done(step, carry):
        c_out(lax.rem(me_col + step, n_col)).wait_send()
        return carry

    lax.fori_loop(1, n_col, c_done, 0)
    direct_phase(n_ba, me_ba, ba_dev, part, out_ref, recv_ba, send_b, recv_b)


def reduce_and_gram(product, sizes, collective_id):
    n_aa, n_ba, n_y, n_core = sizes
    n_col = n_y * n_core
    depth_all, rows = product.shape
    depth = depth_all // (n_core * n_y * n_ba)
    out_rows = rows * n_aa // (n_ba * n_col)
    rows_c = depth_all // n_core
    rows_a = rows_c * 3 // 4
    blk_a = rows_a // n_y
    blk_zb = (rows_c - rows_a) // n_ba
    depth_a = blk_a // n_ba
    depth_b = blk_zb // n_y
    f32 = jnp.float32
    dma = pltpu.SemaphoreType.DMA
    return pl.pallas_call(
        functools.partial(whole_kernel, sizes),
        out_shape=jax.ShapeDtypeStruct((out_rows, rows), f32),
        in_specs=[pl.BlockSpec(memory_space=pltpu.VMEM)],
        out_specs=pl.BlockSpec(memory_space=pltpu.VMEM),
        scratch_shapes=[
            pltpu.VMEM((n_core, rows_c, rows), f32),
            pltpu.VMEM((rows_c, rows), f32),
            pltpu.VMEM((2, n_y - 1, blk_a // 2, rows), f32),
            pltpu.VMEM((2, n_y - 1, blk_a // 2, rows), f32),
            pltpu.VMEM((blk_a, rows), f32),
            pltpu.VMEM((n_ba, blk_zb, rows), f32),
            pltpu.VMEM((blk_zb, rows), f32),
            pltpu.VMEM((n_ba, depth_a, rows), f32),
            pltpu.VMEM((2, n_y - 1, depth_b // 2, rows), f32),
            pltpu.VMEM((2, n_y - 1, depth_b // 2, rows), f32),
            pltpu.VMEM((depth, rows), f32),
            pltpu.VMEM((n_aa, depth, rows), f32),
            pltpu.VMEM((n_aa, rows, depth), f32),
            pltpu.VMEM((n_col, n_ba, out_rows, rows), f32),
            pltpu.VMEM((n_col, n_ba, out_rows, rows), f32),
            pltpu.VMEM((n_ba, out_rows, rows), f32),
            pltpu.VMEM((n_ba, out_rows, rows), f32),
            [dma((n_core,)), dma((n_core,)), dma((2, n_y - 1)), dma((2, n_y - 1)), dma((n_ba,)), dma((n_ba,)),
             dma((n_ba,)), dma((n_ba,)), dma((2, n_y - 1)), dma((2, n_y - 1)),
             dma((n_aa,)), dma((n_aa,)), dma((n_col,)), dma((n_col,)), dma((n_ba,)), dma((n_ba,))],
        ],
        compiler_params=pltpu.CompilerParams(collective_id=collective_id, has_side_effects=True),
    )(product.reshape(n_core, rows_c, rows))


def project(tensor, factor_two, factor_three):
    rank = factor_three.shape[1]
    local_rows = tensor.shape[0]
    local_two = tensor.shape[1]
    partial_value = jnp.dot(
        tensor.reshape(local_rows * local_two, tensor.shape[2]), factor_three, preferred_element_type=jnp.float32
    ).astype(jnp.bfloat16).reshape(local_rows, local_two, rank)
    product = jnp.einsum("jr,ijs->sri", factor_two, partial_value, preferred_element_type=jnp.float32)
    return product.reshape(rank * rank, local_rows)


def body(tensor, factor_two, factor_three):
    rank = factor_three.shape[1]
    product = project(tensor, factor_two, factor_three)
    sizes = (lax.axis_size("aa"), lax.axis_size("ba"), lax.axis_size("y"), lax.axis_size("core"))
    gram_t = reduce_and_gram(product, sizes, 0)
    return gram_t.T * (1.0 / (rank * rank))
def solution(mesh):
    n_core = 2
    shape = mesh.devices.shape
    split = jax.sharding.Mesh(
        mesh.devices.reshape(shape[0], shape[1], shape[2] // n_core, n_core), ("aa", "ba", "y", "core")
    )
    return jax.shard_map(
        body,
        mesh=split,
        in_specs=(P("aa", "ba", ("y", "core")), P("ba", None), P(("y", "core"), None)),
        out_specs=P("aa", ("ba", "y", "core")),
        check_vma=False,
    )
```

```python
import functools

import jax
import jax.numpy as jnp
from jax import lax
from jax.experimental import pallas as pl
from jax.experimental.pallas import tpu as pltpu
from jax.sharding import PartitionSpec as P

MESH = pl.DeviceIdType.MESH


def remote(src, dst, send, recv, dev):
    return pltpu.make_async_remote_copy(
        src_ref=src, dst_ref=dst, send_sem=send, recv_sem=recv, device_id=dev, device_id_type=MESH
    )


def direct_phase(n, me, dev, x_ref, out_ref, recv, send_sem, recv_sem, blk=None):
    def piece(k):
        return x_ref.at[k] if blk is None else x_ref.at[pl.ds(k * blk, blk)]

    def outgoing(peer):
        return remote(piece(peer), recv.at[me], send_sem.at[peer], recv_sem.at[me], dev(peer))

    def incoming(peer):
        return remote(piece(me), recv.at[peer], send_sem.at[peer], recv_sem.at[peer], dev(peer))

    def start(step, carry):
        outgoing(lax.rem(me + step, n)).start()
        return carry

    lax.fori_loop(1, n, start, 0)
    out_ref[...] = piece(me)[...]

    def gather(step, carry):
        peer = lax.rem(me + n - step, n)
        incoming(peer).wait_recv()
        out_ref[...] += recv[peer]
        return carry

    lax.fori_loop(1, n, gather, 0)

    def finish(step, carry):
        outgoing(lax.rem(me + step, n)).wait_send()
        return carry

    lax.fori_loop(1, n, finish, 0)


def direct_start(n, me, dev, x_ref, recv, send_sem, recv_sem, blk):
    def start(step, carry):
        peer = lax.rem(me + step, n)
        remote(x_ref.at[pl.ds(peer * blk, blk)], recv.at[me], send_sem.at[peer], recv_sem.at[me], dev(peer)).start()
        return carry

    lax.fori_loop(1, n, start, 0)


def direct_finish(n, me, dev, x_ref, out_ref, recv, send_sem, recv_sem, blk):
    out_ref[...] = x_ref[pl.ds(me * blk, blk)]

    def gather(step, carry):
        peer = lax.rem(me + n - step, n)
        remote(x_ref.at[pl.ds(me * blk, blk)], recv.at[peer], send_sem.at[peer], recv_sem.at[peer], dev(peer)).wait_recv()
        out_ref[...] += recv[peer]
        return carry

    lax.fori_loop(1, n, gather, 0)

    def finish(step, carry):
        peer = lax.rem(me + step, n)
        remote(x_ref.at[pl.ds(peer * blk, blk)], recv.at[me], send_sem.at[peer], recv_sem.at[me], dev(peer)).wait_send()
        return carry

    lax.fori_loop(1, n, finish, 0)


def ring_flat(n, me, dev, x_ref, out_ref, recv, sendbuf, send_sem, recv_sem, blk):
    right = lax.rem(me + 1, n)
    left = lax.rem(me + n - 1, n)
    half = blk // 2
    towards = (right, left)

    def chunk_sent(d, step):
        return lax.rem(me - step - 1 + 2 * n, n) if d == 0 else lax.rem(me + step + 1, n)

    def rows_of(d, chunk):
        return pl.ds(chunk * blk + d * half, half)

    for step in range(n - 1):
        copies = []
        for d in range(2):
            src = x_ref.at[rows_of(d, chunk_sent(d, 0))] if step == 0 else sendbuf.at[d, step]
            copy = remote(src, recv.at[d, step], send_sem.at[d, step], recv_sem.at[d, step], dev(towards[d]))
            copy.start()
            copies.append(copy)
        for d in range(2):
            copies[d].wait_recv()
            total = recv[d, step] + x_ref[rows_of(d, chunk_sent(d, step + 1))]
            if step < n - 2:
                sendbuf[d, step + 1] = total
            else:
                out_ref[pl.ds(d * half, half)] = total
        for d in range(2):
            copies[d].wait_send()


def ring_phase(n, me, dev, x_ref, out_ref, recv, sendbuf, send_sem, recv_sem):
    right = lax.rem(me + 1, n)
    left = lax.rem(me + n - 1, n)
    half = x_ref.shape[1] // 2
    lanes = (pl.ds(0, half), pl.ds(half, half))
    towards = (right, left)

    def chunk_sent(d, step):
        return lax.rem(me - step - 1 + 2 * n, n) if d == 0 else lax.rem(me + step + 1, n)

    for step in range(n - 1):
        copies = []
        for d in range(2):
            src = x_ref.at[chunk_sent(d, 0), lanes[d]] if step == 0 else sendbuf.at[d, step]
            copy = remote(src, recv.at[d, step], send_sem.at[d, step], recv_sem.at[d, step], dev(towards[d]))
            copy.start()
            copies.append(copy)
        for d in range(2):
            copies[d].wait_recv()
            total = recv[d, step] + x_ref[chunk_sent(d, step + 1), lanes[d]]
            if step < n - 2:
                sendbuf[d, step + 1] = total
            else:
                out_ref[lanes[d]] = total
        for d in range(2):
            copies[d].wait_send()


def whole_kernel(sizes, x_ref, out_ref, core_recv, on_chip, ring_a_recv, ring_a_send, ring_a_out, z_b_recv, z_b_out,
                 z_a_recv, ring_b_recv, ring_b_send, q_buf, gath, gt, terms, recv_col, part, recv_ba, sems):
    n_aa, n_ba, n_y, n_core = sizes
    n_col = n_y * n_core
    per_block = n_ba // n_aa
    out_rows = out_ref.shape[0]
    (s_core, r_core, s_ra, r_ra, s_zb, r_zb, s_za, r_za, s_rb, r_rb, send_g, recv_g, send_c, recv_c, send_b, recv_b) = sems
    me_aa = lax.axis_index("aa")
    me_ba = lax.axis_index("ba")
    me_y = lax.axis_index("y")
    me_core = lax.axis_index("core")
    me_col = me_y * n_core + me_core

    def aa_dev(p):
        return {"aa": p}

    def col_dev(c):
        return {"y": c // n_core, "core": lax.rem(c, n_core)}

    def ba_dev(b):
        return {"ba": b}

    def core_dev(k):
        return {"core": k}

    def y_dev(k):
        return {"y": k}

    barrier = pltpu.get_barrier_semaphore()
    groups = ((n_aa, me_aa, aa_dev), (n_col, me_col, col_dev), (n_ba, me_ba, ba_dev))
    for n, me, dev in groups:
        def greet(step, carry, n=n, me=me, dev=dev):
            pl.semaphore_signal(barrier, inc=1, device_id=dev(lax.rem(me + step, n)), device_id_type=MESH)
            return carry

        lax.fori_loop(1, n, greet, 0)
    pl.semaphore_wait(barrier, n_aa + n_col + n_ba - 3)

    rows_a = on_chip.shape[0] * 3 // 4
    rows_b = on_chip.shape[0] - rows_a
    spans = (pl.ds(0, rows_a), pl.ds(rows_a, rows_b))

    def core_copy(k, src, dst, peer):
        return remote(x_ref.at[src, spans[k]], core_recv.at[dst, spans[k]], s_core.at[k, peer], r_core.at[k, dst],
                      core_dev(peer))

    def core_start(k):
        def start(step, carry):
            peer = lax.rem(me_core + step, n_core)
            core_copy(k, peer, me_core, peer).start()
            return carry

        lax.fori_loop(1, n_core, start, 0)

    def core_finish(k):
        on_chip[spans[k]] = x_ref[me_core, spans[k]]

        def gather(step, carry):
            peer = lax.rem(me_core + n_core - step, n_core)
            core_copy(k, me_core, peer, peer).wait_recv()
            on_chip[spans[k]] += core_recv[peer, spans[k]]
            return carry

        lax.fori_loop(1, n_core, gather, 0)

        def finish(step, carry):
            peer = lax.rem(me_core + step, n_core)
            core_copy(k, peer, me_core, peer).wait_send()
            return carry

        lax.fori_loop(1, n_core, finish, 0)

    core_start(1)
    core_start(0)
    core_finish(1)
    part_a = on_chip.at[spans[0]]
    part_b = on_chip.at[spans[1]]
    blk_zb = rows_b // n_ba
    direct_start(n_ba, me_ba, ba_dev, part_b, z_b_recv, s_zb, r_zb, blk_zb)
    core_finish(0)
    ring_flat(n_y, me_y, y_dev, part_a, ring_a_out, ring_a_recv, ring_a_send, s_ra, r_ra, rows_a // n_y)
    direct_finish(n_ba, me_ba, ba_dev, part_b, z_b_out, z_b_recv, s_zb, r_zb, blk_zb)
    depth_a = ring_a_out.shape[0] // n_ba
    depth_b = blk_zb // n_y
    direct_start(n_ba, me_ba, ba_dev, ring_a_out, z_a_recv, s_za, r_za, depth_a)
    ring_flat(n_y, me_y, y_dev, z_b_out, q_buf.at[pl.ds(depth_a, depth_b)], ring_b_recv, ring_b_send, s_rb, r_rb, depth_b)
    direct_finish(n_ba, me_ba, ba_dev, ring_a_out, q_buf.at[pl.ds(0, depth_a)], z_a_recv, s_za, r_za, depth_a)

    q = q_buf[...]
    gath[me_aa] = q

    def g_out(p):
        return remote(q_buf, gath.at[me_aa], send_g.at[p], recv_g.at[me_aa], aa_dev(p))

    def g_in(p):
        return remote(q_buf, gath.at[p], send_g.at[p], recv_g.at[p], aa_dev(p))

    def g_start(step, carry):
        g_out(lax.rem(me_aa + step, n_aa)).start()
        return carry

    lax.fori_loop(1, n_aa, g_start, 0)

    def g_wait(step, carry):
        g_in(lax.rem(me_aa + n_aa - step, n_aa)).wait_recv()
        return carry

    lax.fori_loop(1, n_aa, g_wait, 0)

    def g_done(step, carry):
        g_out(lax.rem(me_aa + step, n_aa)).wait_send()
        return carry

    lax.fori_loop(1, n_aa, g_done, 0)

    for p in range(n_aa):
        gt[p] = gath[p].T

    def term_block(c):
        pieces = []
        for p in range(n_aa):
            for b2 in range(per_block):
                start = pl.multiple_of(b2 * n_col * out_rows + c * out_rows, out_rows)
                pieces.append(gt[p, pl.ds(start, out_rows), :])
        lhs = jnp.concatenate(pieces, axis=0)
        block = jnp.dot(lhs, q, precision=lax.Precision.HIGHEST, preferred_element_type=jnp.float32)
        return block.reshape(n_ba, out_rows, q.shape[1])

    def c_out(c):
        return remote(terms.at[c], recv_col.at[me_col], send_c.at[c], recv_c.at[me_col], col_dev(c))

    def c_in(c):
        return remote(terms.at[me_col], recv_col.at[c], send_c.at[c], recv_c.at[c], col_dev(c))

    def c_start(step, carry):
        c = lax.rem(me_col + step, n_col)
        terms[c] = term_block(c)
        c_out(c).start()
        return carry

    lax.fori_loop(1, n_col, c_start, 0)
    part[...] = term_block(me_col)

    def c_wait(step, carry):
        peer = lax.rem(me_col + n_col - step, n_col)
        c_in(peer).wait_recv()
        part[...] += recv_col[peer]
        return carry

    lax.fori_loop(1, n_col, c_wait, 0)

    def c_done(step, carry):
        c_out(lax.rem(me_col + step, n_col)).wait_send()
        return carry

    lax.fori_loop(1, n_col, c_done, 0)
    direct_phase(n_ba, me_ba, ba_dev, part, out_ref, recv_ba, send_b, recv_b)


def reduce_and_gram(product, sizes, collective_id):
    n_aa, n_ba, n_y, n_core = sizes
    n_col = n_y * n_core
    depth_all, rows = product.shape
    depth = depth_all // (n_core * n_y * n_ba)
    out_rows = rows * n_aa // (n_ba * n_col)
    rows_c = depth_all // n_core
    rows_a = rows_c * 3 // 4
    blk_a = rows_a // n_y
    blk_zb = (rows_c - rows_a) // n_ba
    depth_a = blk_a // n_ba
    depth_b = blk_zb // n_y
    f32 = jnp.float32
    dma = pltpu.SemaphoreType.DMA
    return pl.pallas_call(
        functools.partial(whole_kernel, sizes),
        out_shape=jax.ShapeDtypeStruct((out_rows, rows), f32),
        in_specs=[pl.BlockSpec(memory_space=pltpu.VMEM)],
        out_specs=pl.BlockSpec(memory_space=pltpu.VMEM),
        scratch_shapes=[
            pltpu.VMEM((n_core, rows_c, rows), f32),
            pltpu.VMEM((rows_c, rows), f32),
            pltpu.VMEM((2, n_y - 1, blk_a // 2, rows), f32),
            pltpu.VMEM((2, n_y - 1, blk_a // 2, rows), f32),
            pltpu.VMEM((blk_a, rows), f32),
            pltpu.VMEM((n_ba, blk_zb, rows), f32),
            pltpu.VMEM((blk_zb, rows), f32),
            pltpu.VMEM((n_ba, depth_a, rows), f32),
            pltpu.VMEM((2, n_y - 1, depth_b // 2, rows), f32),
            pltpu.VMEM((2, n_y - 1, depth_b // 2, rows), f32),
            pltpu.VMEM((depth, rows), f32),
            pltpu.VMEM((n_aa, depth, rows), f32),
            pltpu.VMEM((n_aa, rows, depth), f32),
            pltpu.VMEM((n_col, n_ba, out_rows, rows), f32),
            pltpu.VMEM((n_col, n_ba, out_rows, rows), f32),
            pltpu.VMEM((n_ba, out_rows, rows), f32),
            pltpu.VMEM((n_ba, out_rows, rows), f32),
            [dma((2, n_core)), dma((2, n_core)), dma((2, n_y - 1)), dma((2, n_y - 1)), dma((n_ba,)), dma((n_ba,)),
             dma((n_ba,)), dma((n_ba,)), dma((2, n_y - 1)), dma((2, n_y - 1)),
             dma((n_aa,)), dma((n_aa,)), dma((n_col,)), dma((n_col,)), dma((n_ba,)), dma((n_ba,))],
        ],
        compiler_params=pltpu.CompilerParams(collective_id=collective_id, has_side_effects=True),
    )(product.reshape(n_core, rows_c, rows))


def project(tensor, factor_two, factor_three):
    rank = factor_three.shape[1]
    local_rows = tensor.shape[0]
    local_two = tensor.shape[1]
    partial_value = jnp.dot(
        tensor.reshape(local_rows * local_two, tensor.shape[2]), factor_three, preferred_element_type=jnp.float32
    ).astype(jnp.bfloat16).reshape(local_rows, local_two, rank)
    product = jnp.einsum("jr,ijs->sri", factor_two, partial_value, preferred_element_type=jnp.float32)
    return product.reshape(rank * rank, local_rows)


def body(tensor, factor_two, factor_three):
    rank = factor_three.shape[1]
    product = project(tensor, factor_two, factor_three)
    sizes = (lax.axis_size("aa"), lax.axis_size("ba"), lax.axis_size("y"), lax.axis_size("core"))
    gram_t = reduce_and_gram(product, sizes, 0)
    return gram_t.T * (1.0 / (rank * rank))
def solution(mesh):
    n_core = 2
    shape = mesh.devices.shape
    split = jax.sharding.Mesh(
        mesh.devices.reshape(shape[0], shape[1], shape[2] // n_core, n_core), ("aa", "ba", "y", "core")
    )
    return jax.shard_map(
        body,
        mesh=split,
        in_specs=(P("aa", "ba", ("y", "core")), P("ba", None), P(("y", "core"), None)),
        out_specs=P("aa", ("ba", "y", "core")),
        check_vma=False,
    )
```

```python
import functools

import jax
import jax.numpy as jnp
from jax import lax
from jax.experimental import pallas as pl
from jax.experimental.pallas import tpu as pltpu
from jax.sharding import PartitionSpec as P

MESH = pl.DeviceIdType.MESH


def remote(src, dst, send, recv, dev):
    return pltpu.make_async_remote_copy(
        src_ref=src, dst_ref=dst, send_sem=send, recv_sem=recv, device_id=dev, device_id_type=MESH
    )


def direct_phase(n, me, dev, x_ref, out_ref, recv, send_sem, recv_sem, blk=None):
    def piece(k):
        return x_ref.at[k] if blk is None else x_ref.at[pl.ds(k * blk, blk)]

    def outgoing(peer):
        return remote(piece(peer), recv.at[me], send_sem.at[peer], recv_sem.at[me], dev(peer))

    def incoming(peer):
        return remote(piece(me), recv.at[peer], send_sem.at[peer], recv_sem.at[peer], dev(peer))

    def start(step, carry):
        outgoing(lax.rem(me + step, n)).start()
        return carry

    lax.fori_loop(1, n, start, 0)
    out_ref[...] = piece(me)[...]

    def gather(step, carry):
        peer = lax.rem(me + n - step, n)
        incoming(peer).wait_recv()
        out_ref[...] += recv[peer]
        return carry

    lax.fori_loop(1, n, gather, 0)

    def finish(step, carry):
        outgoing(lax.rem(me + step, n)).wait_send()
        return carry

    lax.fori_loop(1, n, finish, 0)


def direct_start(n, me, dev, x_ref, recv, send_sem, recv_sem, blk):
    def start(step, carry):
        peer = lax.rem(me + step, n)
        remote(x_ref.at[pl.ds(peer * blk, blk)], recv.at[me], send_sem.at[peer], recv_sem.at[me], dev(peer)).start()
        return carry

    lax.fori_loop(1, n, start, 0)


def direct_finish(n, me, dev, x_ref, out_ref, recv, send_sem, recv_sem, blk):
    out_ref[...] = x_ref[pl.ds(me * blk, blk)]

    def gather(step, carry):
        peer = lax.rem(me + n - step, n)
        remote(x_ref.at[pl.ds(me * blk, blk)], recv.at[peer], send_sem.at[peer], recv_sem.at[peer], dev(peer)).wait_recv()
        out_ref[...] += recv[peer]
        return carry

    lax.fori_loop(1, n, gather, 0)

    def finish(step, carry):
        peer = lax.rem(me + step, n)
        remote(x_ref.at[pl.ds(peer * blk, blk)], recv.at[me], send_sem.at[peer], recv_sem.at[me], dev(peer)).wait_send()
        return carry

    lax.fori_loop(1, n, finish, 0)


def ring_flat(n, me, dev, x_ref, out_ref, recv, sendbuf, send_sem, recv_sem, blk):
    lanes = recv.shape[0]
    part = blk // lanes
    towards = (lax.rem(me + 1, n), lax.rem(me + n - 1, n))

    def chunk_sent(d, step):
        return lax.rem(me - step - 1 + 2 * n, n) if d % 2 == 0 else lax.rem(me + step + 1, n)

    def rows_of(d, chunk):
        return pl.ds(chunk * blk + d * part, part)

    def copy(d, step):
        src = x_ref.at[rows_of(d, chunk_sent(d, 0))] if step == 0 else sendbuf.at[d, step]
        return remote(src, recv.at[d, step], send_sem.at[d, step], recv_sem.at[d, step], dev(towards[d % 2]))

    for d in range(lanes):
        copy(d, 0).start()
    for step in range(n - 1):
        for d in range(lanes):
            copy(d, step).wait_recv()
            total = recv[d, step] + x_ref[rows_of(d, chunk_sent(d, step + 1))]
            if step < n - 2:
                sendbuf[d, step + 1] = total
                copy(d, step + 1).start()
            else:
                out_ref[pl.ds(d * part, part)] = total
    for step in range(n - 1):
        for d in range(lanes):
            copy(d, step).wait_send()


def ring_phase(n, me, dev, x_ref, out_ref, recv, sendbuf, send_sem, recv_sem):
    right = lax.rem(me + 1, n)
    left = lax.rem(me + n - 1, n)
    half = x_ref.shape[1] // 2
    lanes = (pl.ds(0, half), pl.ds(half, half))
    towards = (right, left)

    def chunk_sent(d, step):
        return lax.rem(me - step - 1 + 2 * n, n) if d == 0 else lax.rem(me + step + 1, n)

    for step in range(n - 1):
        copies = []
        for d in range(2):
            src = x_ref.at[chunk_sent(d, 0), lanes[d]] if step == 0 else sendbuf.at[d, step]
            copy = remote(src, recv.at[d, step], send_sem.at[d, step], recv_sem.at[d, step], dev(towards[d]))
            copy.start()
            copies.append(copy)
        for d in range(2):
            copies[d].wait_recv()
            total = recv[d, step] + x_ref[chunk_sent(d, step + 1), lanes[d]]
            if step < n - 2:
                sendbuf[d, step + 1] = total
            else:
                out_ref[lanes[d]] = total
        for d in range(2):
            copies[d].wait_send()


def whole_kernel(sizes, x_ref, out_ref, core_recv, on_chip, ring_a_recv, ring_a_send, ring_a_out, z_b_recv, z_b_out,
                 z_a_recv, ring_b_recv, ring_b_send, q_buf, gath, gt, terms, recv_col, part, recv_ba, sems):
    n_aa, n_ba, n_y, n_core = sizes
    n_col = n_y * n_core
    per_block = n_ba // n_aa
    out_rows = out_ref.shape[0]
    (s_core, r_core, s_ra, r_ra, s_zb, r_zb, s_za, r_za, s_rb, r_rb, send_g, recv_g, send_c, recv_c, send_b, recv_b) = sems
    me_aa = lax.axis_index("aa")
    me_ba = lax.axis_index("ba")
    me_y = lax.axis_index("y")
    me_core = lax.axis_index("core")
    me_col = me_y * n_core + me_core

    def aa_dev(p):
        return {"aa": p}

    def col_dev(c):
        return {"y": c // n_core, "core": lax.rem(c, n_core)}

    def ba_dev(b):
        return {"ba": b}

    def core_dev(k):
        return {"core": k}

    def y_dev(k):
        return {"y": k}

    barrier = pltpu.get_barrier_semaphore()
    groups = ((n_aa, me_aa, aa_dev), (n_col, me_col, col_dev), (n_ba, me_ba, ba_dev))
    for n, me, dev in groups:
        def greet(step, carry, n=n, me=me, dev=dev):
            pl.semaphore_signal(barrier, inc=1, device_id=dev(lax.rem(me + step, n)), device_id_type=MESH)
            return carry

        lax.fori_loop(1, n, greet, 0)
    pl.semaphore_wait(barrier, n_aa + n_col + n_ba - 3)

    rows_a = on_chip.shape[0] * 3 // 4
    rows_b = on_chip.shape[0] - rows_a
    spans = (pl.ds(0, rows_a), pl.ds(rows_a, rows_b))

    def core_copy(k, src, dst, peer):
        return remote(x_ref.at[src, spans[k]], core_recv.at[dst, spans[k]], s_core.at[k, peer], r_core.at[k, dst],
                      core_dev(peer))

    def core_start(k):
        def start(step, carry):
            peer = lax.rem(me_core + step, n_core)
            core_copy(k, peer, me_core, peer).start()
            return carry

        lax.fori_loop(1, n_core, start, 0)

    def core_finish(k):
        on_chip[spans[k]] = x_ref[me_core, spans[k]]

        def gather(step, carry):
            peer = lax.rem(me_core + n_core - step, n_core)
            core_copy(k, me_core, peer, peer).wait_recv()
            on_chip[spans[k]] += core_recv[peer, spans[k]]
            return carry

        lax.fori_loop(1, n_core, gather, 0)

        def finish(step, carry):
            peer = lax.rem(me_core + step, n_core)
            core_copy(k, peer, me_core, peer).wait_send()
            return carry

        lax.fori_loop(1, n_core, finish, 0)

    core_start(1)
    core_start(0)
    core_finish(1)
    part_a = on_chip.at[spans[0]]
    part_b = on_chip.at[spans[1]]
    blk_zb = rows_b // n_ba
    direct_start(n_ba, me_ba, ba_dev, part_b, z_b_recv, s_zb, r_zb, blk_zb)
    core_finish(0)
    ring_flat(n_y, me_y, y_dev, part_a, ring_a_out, ring_a_recv, ring_a_send, s_ra, r_ra, rows_a // n_y)
    direct_finish(n_ba, me_ba, ba_dev, part_b, z_b_out, z_b_recv, s_zb, r_zb, blk_zb)
    depth_a = ring_a_out.shape[0] // n_ba
    depth_b = blk_zb // n_y
    direct_start(n_ba, me_ba, ba_dev, ring_a_out, z_a_recv, s_za, r_za, depth_a)
    ring_flat(n_y, me_y, y_dev, z_b_out, q_buf.at[pl.ds(depth_a, depth_b)], ring_b_recv, ring_b_send, s_rb, r_rb, depth_b)
    direct_finish(n_ba, me_ba, ba_dev, ring_a_out, q_buf.at[pl.ds(0, depth_a)], z_a_recv, s_za, r_za, depth_a)

    q = q_buf[...]
    gath[me_aa] = q

    def g_out(p):
        return remote(q_buf, gath.at[me_aa], send_g.at[p], recv_g.at[me_aa], aa_dev(p))

    def g_in(p):
        return remote(q_buf, gath.at[p], send_g.at[p], recv_g.at[p], aa_dev(p))

    def g_start(step, carry):
        g_out(lax.rem(me_aa + step, n_aa)).start()
        return carry

    lax.fori_loop(1, n_aa, g_start, 0)

    def g_wait(step, carry):
        g_in(lax.rem(me_aa + n_aa - step, n_aa)).wait_recv()
        return carry

    lax.fori_loop(1, n_aa, g_wait, 0)

    def g_done(step, carry):
        g_out(lax.rem(me_aa + step, n_aa)).wait_send()
        return carry

    lax.fori_loop(1, n_aa, g_done, 0)

    for p in range(n_aa):
        gt[p] = gath[p].T

    def term_block(c):
        pieces = []
        for p in range(n_aa):
            for b2 in range(per_block):
                start = pl.multiple_of(b2 * n_col * out_rows + c * out_rows, out_rows)
                pieces.append(gt[p, pl.ds(start, out_rows), :])
        lhs = jnp.concatenate(pieces, axis=0)
        block = jnp.dot(lhs, q, precision=lax.Precision.HIGHEST, preferred_element_type=jnp.float32)
        return block.reshape(n_ba, out_rows, q.shape[1])

    def c_out(c):
        return remote(terms.at[c], recv_col.at[me_col], send_c.at[c], recv_c.at[me_col], col_dev(c))

    def c_in(c):
        return remote(terms.at[me_col], recv_col.at[c], send_c.at[c], recv_c.at[c], col_dev(c))

    def c_start(step, carry):
        c = lax.rem(me_col + step, n_col)
        terms[c] = term_block(c)
        c_out(c).start()
        return carry

    lax.fori_loop(1, n_col, c_start, 0)
    part[...] = term_block(me_col)

    def c_wait(step, carry):
        peer = lax.rem(me_col + n_col - step, n_col)
        c_in(peer).wait_recv()
        part[...] += recv_col[peer]
        return carry

    lax.fori_loop(1, n_col, c_wait, 0)

    def c_done(step, carry):
        c_out(lax.rem(me_col + step, n_col)).wait_send()
        return carry

    lax.fori_loop(1, n_col, c_done, 0)
    direct_phase(n_ba, me_ba, ba_dev, part, out_ref, recv_ba, send_b, recv_b)


def reduce_and_gram(product, sizes, collective_id):
    n_aa, n_ba, n_y, n_core = sizes
    n_col = n_y * n_core
    depth_all, rows = product.shape
    depth = depth_all // (n_core * n_y * n_ba)
    out_rows = rows * n_aa // (n_ba * n_col)
    rows_c = depth_all // n_core
    rows_a = rows_c * 3 // 4
    blk_a = rows_a // n_y
    blk_zb = (rows_c - rows_a) // n_ba
    depth_a = blk_a // n_ba
    depth_b = blk_zb // n_y
    f32 = jnp.float32
    dma = pltpu.SemaphoreType.DMA
    return pl.pallas_call(
        functools.partial(whole_kernel, sizes),
        out_shape=jax.ShapeDtypeStruct((out_rows, rows), f32),
        in_specs=[pl.BlockSpec(memory_space=pltpu.VMEM)],
        out_specs=pl.BlockSpec(memory_space=pltpu.VMEM),
        scratch_shapes=[
            pltpu.VMEM((n_core, rows_c, rows), f32),
            pltpu.VMEM((rows_c, rows), f32),
            pltpu.VMEM((4, n_y - 1, blk_a // 4, rows), f32),
            pltpu.VMEM((4, n_y - 1, blk_a // 4, rows), f32),
            pltpu.VMEM((blk_a, rows), f32),
            pltpu.VMEM((n_ba, blk_zb, rows), f32),
            pltpu.VMEM((blk_zb, rows), f32),
            pltpu.VMEM((n_ba, depth_a, rows), f32),
            pltpu.VMEM((2, n_y - 1, depth_b // 2, rows), f32),
            pltpu.VMEM((2, n_y - 1, depth_b // 2, rows), f32),
            pltpu.VMEM((depth, rows), f32),
            pltpu.VMEM((n_aa, depth, rows), f32),
            pltpu.VMEM((n_aa, rows, depth), f32),
            pltpu.VMEM((n_col, n_ba, out_rows, rows), f32),
            pltpu.VMEM((n_col, n_ba, out_rows, rows), f32),
            pltpu.VMEM((n_ba, out_rows, rows), f32),
            pltpu.VMEM((n_ba, out_rows, rows), f32),
            [dma((2, n_core)), dma((2, n_core)), dma((4, n_y - 1)), dma((4, n_y - 1)), dma((n_ba,)), dma((n_ba,)),
             dma((n_ba,)), dma((n_ba,)), dma((2, n_y - 1)), dma((2, n_y - 1)),
             dma((n_aa,)), dma((n_aa,)), dma((n_col,)), dma((n_col,)), dma((n_ba,)), dma((n_ba,))],
        ],
        compiler_params=pltpu.CompilerParams(collective_id=collective_id, has_side_effects=True),
    )(product.reshape(n_core, rows_c, rows))


def project(tensor, factor_two, factor_three):
    rank = factor_three.shape[1]
    local_rows = tensor.shape[0]
    local_two = tensor.shape[1]
    partial_value = jnp.dot(
        tensor.reshape(local_rows * local_two, tensor.shape[2]), factor_three, preferred_element_type=jnp.float32
    ).astype(jnp.bfloat16).reshape(local_rows, local_two, rank)
    product = jnp.einsum("jr,ijs->sri", factor_two, partial_value, preferred_element_type=jnp.float32)
    return product.reshape(rank * rank, local_rows)


def body(tensor, factor_two, factor_three):
    rank = factor_three.shape[1]
    product = project(tensor, factor_two, factor_three)
    sizes = (lax.axis_size("aa"), lax.axis_size("ba"), lax.axis_size("y"), lax.axis_size("core"))
    gram_t = reduce_and_gram(product, sizes, 0)
    return gram_t.T * (1.0 / (rank * rank))
def solution(mesh):
    n_core = 2
    shape = mesh.devices.shape
    split = jax.sharding.Mesh(
        mesh.devices.reshape(shape[0], shape[1], shape[2] // n_core, n_core), ("aa", "ba", "y", "core")
    )
    return jax.shard_map(
        body,
        mesh=split,
        in_specs=(P("aa", "ba", ("y", "core")), P("ba", None), P(("y", "core"), None)),
        out_specs=P("aa", ("ba", "y", "core")),
        check_vma=False,
    )
```

```python
import functools

import jax
import jax.numpy as jnp
from jax import lax
from jax.experimental import pallas as pl
from jax.experimental.pallas import tpu as pltpu
from jax.sharding import PartitionSpec as P

MESH = pl.DeviceIdType.MESH


def remote(src, dst, send, recv, dev):
    return pltpu.make_async_remote_copy(
        src_ref=src, dst_ref=dst, send_sem=send, recv_sem=recv, device_id=dev, device_id_type=MESH
    )


def direct_phase(n, me, dev, x_ref, out_ref, recv, send_sem, recv_sem, blk=None):
    def piece(k):
        return x_ref.at[k] if blk is None else x_ref.at[pl.ds(k * blk, blk)]

    def outgoing(peer):
        return remote(piece(peer), recv.at[me], send_sem.at[peer], recv_sem.at[me], dev(peer))

    def incoming(peer):
        return remote(piece(me), recv.at[peer], send_sem.at[peer], recv_sem.at[peer], dev(peer))

    def start(step, carry):
        outgoing(lax.rem(me + step, n)).start()
        return carry

    lax.fori_loop(1, n, start, 0)
    out_ref[...] = piece(me)[...]

    def gather(step, carry):
        peer = lax.rem(me + n - step, n)
        incoming(peer).wait_recv()
        out_ref[...] += recv[peer]
        return carry

    lax.fori_loop(1, n, gather, 0)

    def finish(step, carry):
        outgoing(lax.rem(me + step, n)).wait_send()
        return carry

    lax.fori_loop(1, n, finish, 0)


def direct_start(n, me, dev, x_ref, recv, send_sem, recv_sem, blk):
    def start(step, carry):
        peer = lax.rem(me + step, n)
        remote(x_ref.at[pl.ds(peer * blk, blk)], recv.at[me], send_sem.at[peer], recv_sem.at[me], dev(peer)).start()
        return carry

    lax.fori_loop(1, n, start, 0)


def direct_finish(n, me, dev, x_ref, out_ref, recv, send_sem, recv_sem, blk):
    out_ref[...] = x_ref[pl.ds(me * blk, blk)]

    def gather(step, carry):
        peer = lax.rem(me + n - step, n)
        remote(x_ref.at[pl.ds(me * blk, blk)], recv.at[peer], send_sem.at[peer], recv_sem.at[peer], dev(peer)).wait_recv()
        out_ref[...] += recv[peer]
        return carry

    lax.fori_loop(1, n, gather, 0)

    def finish(step, carry):
        peer = lax.rem(me + step, n)
        remote(x_ref.at[pl.ds(peer * blk, blk)], recv.at[me], send_sem.at[peer], recv_sem.at[me], dev(peer)).wait_send()
        return carry

    lax.fori_loop(1, n, finish, 0)


def ring_flat(n, me, dev, x_ref, out_ref, recv, sendbuf, send_sem, recv_sem, blk, ready=None):
    lanes = recv.shape[0]
    part = blk // lanes
    towards = (lax.rem(me + 1, n), lax.rem(me + n - 1, n))

    def chunk_sent(d, step):
        return lax.rem(me - step - 1 + 2 * n, n) if d % 2 == 0 else lax.rem(me + step + 1, n)

    def rows_of(d, chunk):
        return pl.ds(chunk * blk + d * part, part)

    def copy(d, step):
        src = x_ref.at[rows_of(d, chunk_sent(d, 0))] if step == 0 else sendbuf.at[d, step]
        return remote(src, recv.at[d, step], send_sem.at[d, step], recv_sem.at[d, step], dev(towards[d % 2]))

    for d in range(lanes):
        copy(d, 0).start()
    if ready is not None:
        ready()
    for step in range(n - 1):
        for d in range(lanes):
            copy(d, step).wait_recv()
            total = recv[d, step] + x_ref[rows_of(d, chunk_sent(d, step + 1))]
            if step < n - 2:
                sendbuf[d, step + 1] = total
                copy(d, step + 1).start()
            else:
                out_ref[pl.ds(d * part, part)] = total
    for step in range(n - 1):
        for d in range(lanes):
            copy(d, step).wait_send()


def ring_phase(n, me, dev, x_ref, out_ref, recv, sendbuf, send_sem, recv_sem):
    right = lax.rem(me + 1, n)
    left = lax.rem(me + n - 1, n)
    half = x_ref.shape[1] // 2
    lanes = (pl.ds(0, half), pl.ds(half, half))
    towards = (right, left)

    def chunk_sent(d, step):
        return lax.rem(me - step - 1 + 2 * n, n) if d == 0 else lax.rem(me + step + 1, n)

    for step in range(n - 1):
        copies = []
        for d in range(2):
            src = x_ref.at[chunk_sent(d, 0), lanes[d]] if step == 0 else sendbuf.at[d, step]
            copy = remote(src, recv.at[d, step], send_sem.at[d, step], recv_sem.at[d, step], dev(towards[d]))
            copy.start()
            copies.append(copy)
        for d in range(2):
            copies[d].wait_recv()
            total = recv[d, step] + x_ref[chunk_sent(d, step + 1), lanes[d]]
            if step < n - 2:
                sendbuf[d, step + 1] = total
            else:
                out_ref[lanes[d]] = total
        for d in range(2):
            copies[d].wait_send()


def whole_kernel(sizes, x_ref, out_ref, core_recv, on_chip, ring_a_recv, ring_a_send, ring_a_out, z_b_recv, z_b_out,
                 z_a_recv, ring_b_recv, ring_b_send, q_buf, gath, gt, terms, recv_col, part, recv_ba, sems):
    n_aa, n_ba, n_y, n_core = sizes
    n_col = n_y * n_core
    per_block = n_ba // n_aa
    out_rows = out_ref.shape[0]
    (s_core, r_core, s_ra, r_ra, s_zb, r_zb, s_za, r_za, s_rb, r_rb, send_g, recv_g, send_c, recv_c, send_b, recv_b) = sems
    me_aa = lax.axis_index("aa")
    me_ba = lax.axis_index("ba")
    me_y = lax.axis_index("y")
    me_core = lax.axis_index("core")
    me_col = me_y * n_core + me_core

    def aa_dev(p):
        return {"aa": p}

    def col_dev(c):
        return {"y": c // n_core, "core": lax.rem(c, n_core)}

    def ba_dev(b):
        return {"ba": b}

    def core_dev(k):
        return {"core": k}

    def y_dev(k):
        return {"y": k}

    barrier = pltpu.get_barrier_semaphore()
    groups = ((n_aa, me_aa, aa_dev), (n_col, me_col, col_dev), (n_ba, me_ba, ba_dev))
    for n, me, dev in groups:
        def greet(step, carry, n=n, me=me, dev=dev):
            pl.semaphore_signal(barrier, inc=1, device_id=dev(lax.rem(me + step, n)), device_id_type=MESH)
            return carry

        lax.fori_loop(1, n, greet, 0)
    pl.semaphore_wait(barrier, n_aa + n_col + n_ba - 3)

    rows_a = on_chip.shape[0] * 3 // 4
    rows_b = on_chip.shape[0] - rows_a
    blk_a = rows_a // n_y
    firsts = sorted({(n_y - 1) % n_y, 1 % n_y})
    offsets = firsts + [o for o in range(n_y) if o not in firsts]
    spans = [pl.ds(lax.rem(me_y + o, n_y) * blk_a, blk_a) for o in offsets] + [pl.ds(rows_a, rows_b)]

    def core_copy(k, src, dst, peer):
        return remote(x_ref.at[src, spans[k]], core_recv.at[dst, spans[k]], s_core.at[k, peer], r_core.at[k, dst],
                      core_dev(peer))

    def core_start(k):
        def start(step, carry):
            peer = lax.rem(me_core + step, n_core)
            core_copy(k, peer, me_core, peer).start()
            return carry

        lax.fori_loop(1, n_core, start, 0)

    def core_finish(k):
        on_chip[spans[k]] = x_ref[me_core, spans[k]]

        def gather(step, carry):
            peer = lax.rem(me_core + n_core - step, n_core)
            core_copy(k, me_core, peer, peer).wait_recv()
            on_chip[spans[k]] += core_recv[peer, spans[k]]
            return carry

        lax.fori_loop(1, n_core, gather, 0)

        def finish(step, carry):
            peer = lax.rem(me_core + step, n_core)
            core_copy(k, peer, me_core, peer).wait_send()
            return carry

        lax.fori_loop(1, n_core, finish, 0)

    for k in [n_y] + list(range(n_y)):
        core_start(k)
    core_finish(n_y)
    part_a = on_chip.at[pl.ds(0, rows_a)]
    part_b = on_chip.at[pl.ds(rows_a, rows_b)]
    blk_zb = rows_b // n_ba
    direct_start(n_ba, me_ba, ba_dev, part_b, z_b_recv, s_zb, r_zb, blk_zb)
    for k in range(len(firsts)):
        core_finish(k)

    def rest_ready():
        for k in range(len(firsts), n_y):
            core_finish(k)

    ring_flat(n_y, me_y, y_dev, part_a, ring_a_out, ring_a_recv, ring_a_send, s_ra, r_ra, blk_a, ready=rest_ready)
    direct_finish(n_ba, me_ba, ba_dev, part_b, z_b_out, z_b_recv, s_zb, r_zb, blk_zb)
    depth_a = ring_a_out.shape[0] // n_ba
    depth_b = blk_zb // n_y
    direct_start(n_ba, me_ba, ba_dev, ring_a_out, z_a_recv, s_za, r_za, depth_a)
    ring_flat(n_y, me_y, y_dev, z_b_out, q_buf.at[pl.ds(depth_a, depth_b)], ring_b_recv, ring_b_send, s_rb, r_rb, depth_b)
    direct_finish(n_ba, me_ba, ba_dev, ring_a_out, q_buf.at[pl.ds(0, depth_a)], z_a_recv, s_za, r_za, depth_a)

    q = q_buf[...]
    gath[me_aa] = q

    def g_out(p):
        return remote(q_buf, gath.at[me_aa], send_g.at[p], recv_g.at[me_aa], aa_dev(p))

    def g_in(p):
        return remote(q_buf, gath.at[p], send_g.at[p], recv_g.at[p], aa_dev(p))

    def g_start(step, carry):
        g_out(lax.rem(me_aa + step, n_aa)).start()
        return carry

    lax.fori_loop(1, n_aa, g_start, 0)

    def g_wait(step, carry):
        g_in(lax.rem(me_aa + n_aa - step, n_aa)).wait_recv()
        return carry

    lax.fori_loop(1, n_aa, g_wait, 0)

    def g_done(step, carry):
        g_out(lax.rem(me_aa + step, n_aa)).wait_send()
        return carry

    lax.fori_loop(1, n_aa, g_done, 0)

    for p in range(n_aa):
        gt[p] = gath[p].T

    def term_block(c):
        pieces = []
        for p in range(n_aa):
            for b2 in range(per_block):
                start = pl.multiple_of(b2 * n_col * out_rows + c * out_rows, out_rows)
                pieces.append(gt[p, pl.ds(start, out_rows), :])
        lhs = jnp.concatenate(pieces, axis=0)
        block = jnp.dot(lhs, q, precision=lax.Precision.HIGHEST, preferred_element_type=jnp.float32)
        return block.reshape(n_ba, out_rows, q.shape[1])

    def c_out(c):
        return remote(terms.at[c], recv_col.at[me_col], send_c.at[c], recv_c.at[me_col], col_dev(c))

    def c_in(c):
        return remote(terms.at[me_col], recv_col.at[c], send_c.at[c], recv_c.at[c], col_dev(c))

    def c_start(step, carry):
        c = lax.rem(me_col + step, n_col)
        terms[c] = term_block(c)
        c_out(c).start()
        return carry

    lax.fori_loop(1, n_col, c_start, 0)
    part[...] = term_block(me_col)

    def c_wait(step, carry):
        peer = lax.rem(me_col + n_col - step, n_col)
        c_in(peer).wait_recv()
        part[...] += recv_col[peer]
        return carry

    lax.fori_loop(1, n_col, c_wait, 0)

    def c_done(step, carry):
        c_out(lax.rem(me_col + step, n_col)).wait_send()
        return carry

    lax.fori_loop(1, n_col, c_done, 0)
    direct_phase(n_ba, me_ba, ba_dev, part, out_ref, recv_ba, send_b, recv_b)


def reduce_and_gram(product, sizes, collective_id):
    n_aa, n_ba, n_y, n_core = sizes
    n_col = n_y * n_core
    depth_all, rows = product.shape
    depth = depth_all // (n_core * n_y * n_ba)
    out_rows = rows * n_aa // (n_ba * n_col)
    rows_c = depth_all // n_core
    rows_a = rows_c * 3 // 4
    blk_a = rows_a // n_y
    blk_zb = (rows_c - rows_a) // n_ba
    depth_a = blk_a // n_ba
    depth_b = blk_zb // n_y
    f32 = jnp.float32
    dma = pltpu.SemaphoreType.DMA
    return pl.pallas_call(
        functools.partial(whole_kernel, sizes),
        out_shape=jax.ShapeDtypeStruct((out_rows, rows), f32),
        in_specs=[pl.BlockSpec(memory_space=pltpu.VMEM)],
        out_specs=pl.BlockSpec(memory_space=pltpu.VMEM),
        scratch_shapes=[
            pltpu.VMEM((n_core, rows_c, rows), f32),
            pltpu.VMEM((rows_c, rows), f32),
            pltpu.VMEM((4, n_y - 1, blk_a // 4, rows), f32),
            pltpu.VMEM((4, n_y - 1, blk_a // 4, rows), f32),
            pltpu.VMEM((blk_a, rows), f32),
            pltpu.VMEM((n_ba, blk_zb, rows), f32),
            pltpu.VMEM((blk_zb, rows), f32),
            pltpu.VMEM((n_ba, depth_a, rows), f32),
            pltpu.VMEM((2, n_y - 1, depth_b // 2, rows), f32),
            pltpu.VMEM((2, n_y - 1, depth_b // 2, rows), f32),
            pltpu.VMEM((depth, rows), f32),
            pltpu.VMEM((n_aa, depth, rows), f32),
            pltpu.VMEM((n_aa, rows, depth), f32),
            pltpu.VMEM((n_col, n_ba, out_rows, rows), f32),
            pltpu.VMEM((n_col, n_ba, out_rows, rows), f32),
            pltpu.VMEM((n_ba, out_rows, rows), f32),
            pltpu.VMEM((n_ba, out_rows, rows), f32),
            [dma((n_y + 1, n_core)), dma((n_y + 1, n_core)), dma((4, n_y - 1)), dma((4, n_y - 1)), dma((n_ba,)), dma((n_ba,)),
             dma((n_ba,)), dma((n_ba,)), dma((2, n_y - 1)), dma((2, n_y - 1)),
             dma((n_aa,)), dma((n_aa,)), dma((n_col,)), dma((n_col,)), dma((n_ba,)), dma((n_ba,))],
        ],
        compiler_params=pltpu.CompilerParams(collective_id=collective_id, has_side_effects=True),
    )(product.reshape(n_core, rows_c, rows))


def project(tensor, factor_two, factor_three):
    rank = factor_three.shape[1]
    local_rows = tensor.shape[0]
    local_two = tensor.shape[1]
    partial_value = jnp.dot(
        tensor.reshape(local_rows * local_two, tensor.shape[2]), factor_three, preferred_element_type=jnp.float32
    ).astype(jnp.bfloat16).reshape(local_rows, local_two, rank)
    product = jnp.einsum("jr,ijs->sri", factor_two, partial_value, preferred_element_type=jnp.float32)
    return product.reshape(rank * rank, local_rows)


def body(tensor, factor_two, factor_three):
    rank = factor_three.shape[1]
    product = project(tensor, factor_two, factor_three)
    sizes = (lax.axis_size("aa"), lax.axis_size("ba"), lax.axis_size("y"), lax.axis_size("core"))
    gram_t = reduce_and_gram(product, sizes, 0)
    return gram_t.T * (1.0 / (rank * rank))
def solution(mesh):
    n_core = 2
    shape = mesh.devices.shape
    split = jax.sharding.Mesh(
        mesh.devices.reshape(shape[0], shape[1], shape[2] // n_core, n_core), ("aa", "ba", "y", "core")
    )
    return jax.shard_map(
        body,
        mesh=split,
        in_specs=(P("aa", "ba", ("y", "core")), P("ba", None), P(("y", "core"), None)),
        out_specs=P("aa", ("ba", "y", "core")),
        check_vma=False,
    )
```

```python
import functools

import jax
import jax.numpy as jnp
from jax import lax
from jax.experimental import pallas as pl
from jax.experimental.pallas import tpu as pltpu
from jax.sharding import PartitionSpec as P

MESH = pl.DeviceIdType.MESH


def remote(src, dst, send, recv, dev):
    return pltpu.make_async_remote_copy(
        src_ref=src, dst_ref=dst, send_sem=send, recv_sem=recv, device_id=dev, device_id_type=MESH
    )


def direct_phase(n, me, dev, x_ref, out_ref, recv, send_sem, recv_sem, blk=None):
    def piece(k):
        return x_ref.at[k] if blk is None else x_ref.at[pl.ds(k * blk, blk)]

    def outgoing(peer):
        return remote(piece(peer), recv.at[me], send_sem.at[peer], recv_sem.at[me], dev(peer))

    def incoming(peer):
        return remote(piece(me), recv.at[peer], send_sem.at[peer], recv_sem.at[peer], dev(peer))

    def start(step, carry):
        outgoing(lax.rem(me + step, n)).start()
        return carry

    lax.fori_loop(1, n, start, 0)
    out_ref[...] = piece(me)[...]

    def gather(step, carry):
        peer = lax.rem(me + n - step, n)
        incoming(peer).wait_recv()
        out_ref[...] += recv[peer]
        return carry

    lax.fori_loop(1, n, gather, 0)

    def finish(step, carry):
        outgoing(lax.rem(me + step, n)).wait_send()
        return carry

    lax.fori_loop(1, n, finish, 0)


def direct_start(n, me, dev, x_ref, recv, send_sem, recv_sem, blk):
    def start(step, carry):
        peer = lax.rem(me + step, n)
        remote(x_ref.at[pl.ds(peer * blk, blk)], recv.at[me], send_sem.at[peer], recv_sem.at[me], dev(peer)).start()
        return carry

    lax.fori_loop(1, n, start, 0)


def direct_finish(n, me, dev, x_ref, out_ref, recv, send_sem, recv_sem, blk):
    out_ref[...] = x_ref[pl.ds(me * blk, blk)]

    def gather(step, carry):
        peer = lax.rem(me + n - step, n)
        remote(x_ref.at[pl.ds(me * blk, blk)], recv.at[peer], send_sem.at[peer], recv_sem.at[peer], dev(peer)).wait_recv()
        out_ref[...] += recv[peer]
        return carry

    lax.fori_loop(1, n, gather, 0)

    def finish(step, carry):
        peer = lax.rem(me + step, n)
        remote(x_ref.at[pl.ds(peer * blk, blk)], recv.at[me], send_sem.at[peer], recv_sem.at[me], dev(peer)).wait_send()
        return carry

    lax.fori_loop(1, n, finish, 0)


def ring_flat(n, me, dev, x_ref, out_ref, recv, sendbuf, send_sem, recv_sem, blk, ready=None, lane_done=None):
    lanes = recv.shape[0]
    part = blk // lanes
    towards = (lax.rem(me + 1, n), lax.rem(me + n - 1, n))

    def chunk_sent(d, step):
        return lax.rem(me - step - 1 + 2 * n, n) if d % 2 == 0 else lax.rem(me + step + 1, n)

    def rows_of(d, chunk):
        return pl.ds(chunk * blk + d * part, part)

    def copy(d, step):
        src = x_ref.at[rows_of(d, chunk_sent(d, 0))] if step == 0 else sendbuf.at[d, step]
        return remote(src, recv.at[d, step], send_sem.at[d, step], recv_sem.at[d, step], dev(towards[d % 2]))

    for d in range(lanes):
        copy(d, 0).start()
    if ready is not None:
        ready()
    for step in range(n - 1):
        for d in range(lanes):
            copy(d, step).wait_recv()
            total = recv[d, step] + x_ref[rows_of(d, chunk_sent(d, step + 1))]
            if step < n - 2:
                sendbuf[d, step + 1] = total
                copy(d, step + 1).start()
            else:
                out_ref[pl.ds(d * part, part)] = total
                if lane_done is not None:
                    lane_done(d, part)
    for step in range(n - 1):
        for d in range(lanes):
            copy(d, step).wait_send()


def ring_phase(n, me, dev, x_ref, out_ref, recv, sendbuf, send_sem, recv_sem):
    right = lax.rem(me + 1, n)
    left = lax.rem(me + n - 1, n)
    half = x_ref.shape[1] // 2
    lanes = (pl.ds(0, half), pl.ds(half, half))
    towards = (right, left)

    def chunk_sent(d, step):
        return lax.rem(me - step - 1 + 2 * n, n) if d == 0 else lax.rem(me + step + 1, n)

    for step in range(n - 1):
        copies = []
        for d in range(2):
            src = x_ref.at[chunk_sent(d, 0), lanes[d]] if step == 0 else sendbuf.at[d, step]
            copy = remote(src, recv.at[d, step], send_sem.at[d, step], recv_sem.at[d, step], dev(towards[d]))
            copy.start()
            copies.append(copy)
        for d in range(2):
            copies[d].wait_recv()
            total = recv[d, step] + x_ref[chunk_sent(d, step + 1), lanes[d]]
            if step < n - 2:
                sendbuf[d, step + 1] = total
            else:
                out_ref[lanes[d]] = total
        for d in range(2):
            copies[d].wait_send()


def whole_kernel(sizes, x_ref, out_ref, core_recv, on_chip, ring_a_recv, ring_a_send, ring_a_out, z_b_recv, z_b_out,
                 z_a_recv, ring_b_recv, ring_b_send, q_buf, gath, gt, terms, recv_col, part, recv_ba, sems):
    n_aa, n_ba, n_y, n_core = sizes
    n_col = n_y * n_core
    per_block = n_ba // n_aa
    out_rows = out_ref.shape[0]
    (s_core, r_core, s_ra, r_ra, s_zb, r_zb, s_za, r_za, s_rb, r_rb, send_g, recv_g, send_c, recv_c, send_b, recv_b) = sems
    me_aa = lax.axis_index("aa")
    me_ba = lax.axis_index("ba")
    me_y = lax.axis_index("y")
    me_core = lax.axis_index("core")
    me_col = me_y * n_core + me_core

    def aa_dev(p):
        return {"aa": p}

    def col_dev(c):
        return {"y": c // n_core, "core": lax.rem(c, n_core)}

    def ba_dev(b):
        return {"ba": b}

    def core_dev(k):
        return {"core": k}

    def y_dev(k):
        return {"y": k}

    barrier = pltpu.get_barrier_semaphore()
    groups = ((n_aa, me_aa, aa_dev), (n_col, me_col, col_dev), (n_ba, me_ba, ba_dev))
    for n, me, dev in groups:
        def greet(step, carry, n=n, me=me, dev=dev):
            pl.semaphore_signal(barrier, inc=1, device_id=dev(lax.rem(me + step, n)), device_id_type=MESH)
            return carry

        lax.fori_loop(1, n, greet, 0)
    pl.semaphore_wait(barrier, n_aa + n_col + n_ba - 3)

    rows_a = on_chip.shape[0] * 3 // 4
    rows_b = on_chip.shape[0] - rows_a
    blk_a = rows_a // n_y
    firsts = sorted({(n_y - 1) % n_y, 1 % n_y})
    offsets = firsts + [o for o in range(n_y) if o not in firsts]
    spans = [pl.ds(lax.rem(me_y + o, n_y) * blk_a, blk_a) for o in offsets] + [pl.ds(rows_a, rows_b)]

    def core_copy(k, src, dst, peer):
        return remote(x_ref.at[src, spans[k]], core_recv.at[dst, spans[k]], s_core.at[k, peer], r_core.at[k, dst],
                      core_dev(peer))

    def core_start(k):
        def start(step, carry):
            peer = lax.rem(me_core + step, n_core)
            core_copy(k, peer, me_core, peer).start()
            return carry

        lax.fori_loop(1, n_core, start, 0)

    def core_finish(k):
        on_chip[spans[k]] = x_ref[me_core, spans[k]]

        def gather(step, carry):
            peer = lax.rem(me_core + n_core - step, n_core)
            core_copy(k, me_core, peer, peer).wait_recv()
            on_chip[spans[k]] += core_recv[peer, spans[k]]
            return carry

        lax.fori_loop(1, n_core, gather, 0)

        def finish(step, carry):
            peer = lax.rem(me_core + step, n_core)
            core_copy(k, peer, me_core, peer).wait_send()
            return carry

        lax.fori_loop(1, n_core, finish, 0)

    for k in [n_y] + list(range(n_y)):
        core_start(k)
    core_finish(n_y)
    part_a = on_chip.at[pl.ds(0, rows_a)]
    part_b = on_chip.at[pl.ds(rows_a, rows_b)]
    blk_zb = rows_b // n_ba
    direct_start(n_ba, me_ba, ba_dev, part_b, z_b_recv, s_zb, r_zb, blk_zb)
    for k in range(len(firsts)):
        core_finish(k)

    def rest_ready():
        for k in range(len(firsts), n_y):
            core_finish(k)

    depth_a = ring_a_out.shape[0] // n_ba

    def send_lane(d, part):
        for p in range(d * part // depth_a, (d + 1) * part // depth_a):
            @pl.when(me_ba != p)
            def _():
                remote(ring_a_out.at[pl.ds(p * depth_a, depth_a)], z_a_recv.at[me_ba], s_za.at[p], r_za.at[me_ba],
                       ba_dev(p)).start()

    ring_flat(n_y, me_y, y_dev, part_a, ring_a_out, ring_a_recv, ring_a_send, s_ra, r_ra, blk_a, ready=rest_ready,
              lane_done=send_lane)
    direct_finish(n_ba, me_ba, ba_dev, part_b, z_b_out, z_b_recv, s_zb, r_zb, blk_zb)
    depth_b = blk_zb // n_y
    ring_flat(n_y, me_y, y_dev, z_b_out, q_buf.at[pl.ds(depth_a, depth_b)], ring_b_recv, ring_b_send, s_rb, r_rb, depth_b)
    direct_finish(n_ba, me_ba, ba_dev, ring_a_out, q_buf.at[pl.ds(0, depth_a)], z_a_recv, s_za, r_za, depth_a)

    q = q_buf[...]
    gath[me_aa] = q

    def g_out(p):
        return remote(q_buf, gath.at[me_aa], send_g.at[p], recv_g.at[me_aa], aa_dev(p))

    def g_in(p):
        return remote(q_buf, gath.at[p], send_g.at[p], recv_g.at[p], aa_dev(p))

    def g_start(step, carry):
        g_out(lax.rem(me_aa + step, n_aa)).start()
        return carry

    lax.fori_loop(1, n_aa, g_start, 0)

    def g_wait(step, carry):
        g_in(lax.rem(me_aa + n_aa - step, n_aa)).wait_recv()
        return carry

    lax.fori_loop(1, n_aa, g_wait, 0)

    def g_done(step, carry):
        g_out(lax.rem(me_aa + step, n_aa)).wait_send()
        return carry

    lax.fori_loop(1, n_aa, g_done, 0)

    for p in range(n_aa):
        gt[p] = gath[p].T

    def term_block(c):
        pieces = []
        for p in range(n_aa):
            for b2 in range(per_block):
                start = pl.multiple_of(b2 * n_col * out_rows + c * out_rows, out_rows)
                pieces.append(gt[p, pl.ds(start, out_rows), :])
        lhs = jnp.concatenate(pieces, axis=0)
        block = jnp.dot(lhs, q, precision=lax.Precision.HIGHEST, preferred_element_type=jnp.float32)
        return block.reshape(n_ba, out_rows, q.shape[1])

    def c_out(c):
        return remote(terms.at[c], recv_col.at[me_col], send_c.at[c], recv_c.at[me_col], col_dev(c))

    def c_in(c):
        return remote(terms.at[me_col], recv_col.at[c], send_c.at[c], recv_c.at[c], col_dev(c))

    def c_start(step, carry):
        c = lax.rem(me_col + step, n_col)
        terms[c] = term_block(c)
        c_out(c).start()
        return carry

    lax.fori_loop(1, n_col, c_start, 0)
    part[...] = term_block(me_col)

    def c_wait(step, carry):
        peer = lax.rem(me_col + n_col - step, n_col)
        c_in(peer).wait_recv()
        part[...] += recv_col[peer]
        return carry

    lax.fori_loop(1, n_col, c_wait, 0)

    def c_done(step, carry):
        c_out(lax.rem(me_col + step, n_col)).wait_send()
        return carry

    lax.fori_loop(1, n_col, c_done, 0)
    direct_phase(n_ba, me_ba, ba_dev, part, out_ref, recv_ba, send_b, recv_b)


def reduce_and_gram(product, sizes, collective_id):
    n_aa, n_ba, n_y, n_core = sizes
    n_col = n_y * n_core
    depth_all, rows = product.shape
    depth = depth_all // (n_core * n_y * n_ba)
    out_rows = rows * n_aa // (n_ba * n_col)
    rows_c = depth_all // n_core
    rows_a = rows_c * 3 // 4
    blk_a = rows_a // n_y
    blk_zb = (rows_c - rows_a) // n_ba
    depth_a = blk_a // n_ba
    depth_b = blk_zb // n_y
    f32 = jnp.float32
    dma = pltpu.SemaphoreType.DMA
    return pl.pallas_call(
        functools.partial(whole_kernel, sizes),
        out_shape=jax.ShapeDtypeStruct((out_rows, rows), f32),
        in_specs=[pl.BlockSpec(memory_space=pltpu.VMEM)],
        out_specs=pl.BlockSpec(memory_space=pltpu.VMEM),
        scratch_shapes=[
            pltpu.VMEM((n_core, rows_c, rows), f32),
            pltpu.VMEM((rows_c, rows), f32),
            pltpu.VMEM((4, n_y - 1, blk_a // 4, rows), f32),
            pltpu.VMEM((4, n_y - 1, blk_a // 4, rows), f32),
            pltpu.VMEM((blk_a, rows), f32),
            pltpu.VMEM((n_ba, blk_zb, rows), f32),
            pltpu.VMEM((blk_zb, rows), f32),
            pltpu.VMEM((n_ba, depth_a, rows), f32),
            pltpu.VMEM((2, n_y - 1, depth_b // 2, rows), f32),
            pltpu.VMEM((2, n_y - 1, depth_b // 2, rows), f32),
            pltpu.VMEM((depth, rows), f32),
            pltpu.VMEM((n_aa, depth, rows), f32),
            pltpu.VMEM((n_aa, rows, depth), f32),
            pltpu.VMEM((n_col, n_ba, out_rows, rows), f32),
            pltpu.VMEM((n_col, n_ba, out_rows, rows), f32),
            pltpu.VMEM((n_ba, out_rows, rows), f32),
            pltpu.VMEM((n_ba, out_rows, rows), f32),
            [dma((n_y + 1, n_core)), dma((n_y + 1, n_core)), dma((4, n_y - 1)), dma((4, n_y - 1)), dma((n_ba,)), dma((n_ba,)),
             dma((n_ba,)), dma((n_ba,)), dma((2, n_y - 1)), dma((2, n_y - 1)),
             dma((n_aa,)), dma((n_aa,)), dma((n_col,)), dma((n_col,)), dma((n_ba,)), dma((n_ba,))],
        ],
        compiler_params=pltpu.CompilerParams(collective_id=collective_id, has_side_effects=True),
    )(product.reshape(n_core, rows_c, rows))


def project(tensor, factor_two, factor_three):
    rank = factor_three.shape[1]
    local_rows = tensor.shape[0]
    local_two = tensor.shape[1]
    partial_value = jnp.dot(
        tensor.reshape(local_rows * local_two, tensor.shape[2]), factor_three, preferred_element_type=jnp.float32
    ).astype(jnp.bfloat16).reshape(local_rows, local_two, rank)
    product = jnp.einsum("jr,ijs->sri", factor_two, partial_value, preferred_element_type=jnp.float32)
    return product.reshape(rank * rank, local_rows)


def body(tensor, factor_two, factor_three):
    rank = factor_three.shape[1]
    product = project(tensor, factor_two, factor_three)
    sizes = (lax.axis_size("aa"), lax.axis_size("ba"), lax.axis_size("y"), lax.axis_size("core"))
    gram_t = reduce_and_gram(product, sizes, 0)
    return gram_t.T * (1.0 / (rank * rank))
def solution(mesh):
    n_core = 2
    shape = mesh.devices.shape
    split = jax.sharding.Mesh(
        mesh.devices.reshape(shape[0], shape[1], shape[2] // n_core, n_core), ("aa", "ba", "y", "core")
    )
    return jax.shard_map(
        body,
        mesh=split,
        in_specs=(P("aa", "ba", ("y", "core")), P("ba", None), P(("y", "core"), None)),
        out_specs=P("aa", ("ba", "y", "core")),
        check_vma=False,
    )
```

```python
import functools

import jax
import jax.numpy as jnp
from jax import lax
from jax.experimental import pallas as pl
from jax.experimental.pallas import tpu as pltpu
from jax.sharding import PartitionSpec as P

MESH = pl.DeviceIdType.MESH


def remote(src, dst, send, recv, dev):
    return pltpu.make_async_remote_copy(
        src_ref=src, dst_ref=dst, send_sem=send, recv_sem=recv, device_id=dev, device_id_type=MESH
    )


def direct_phase(n, me, dev, x_ref, out_ref, recv, send_sem, recv_sem, blk=None):
    def piece(k):
        return x_ref.at[k] if blk is None else x_ref.at[pl.ds(k * blk, blk)]

    def outgoing(peer):
        return remote(piece(peer), recv.at[me], send_sem.at[peer], recv_sem.at[me], dev(peer))

    def incoming(peer):
        return remote(piece(me), recv.at[peer], send_sem.at[peer], recv_sem.at[peer], dev(peer))

    def start(step, carry):
        outgoing(lax.rem(me + step, n)).start()
        return carry

    lax.fori_loop(1, n, start, 0)
    out_ref[...] = piece(me)[...]

    def gather(step, carry):
        peer = lax.rem(me + n - step, n)
        incoming(peer).wait_recv()
        out_ref[...] += recv[peer]
        return carry

    lax.fori_loop(1, n, gather, 0)

    def finish(step, carry):
        outgoing(lax.rem(me + step, n)).wait_send()
        return carry

    lax.fori_loop(1, n, finish, 0)


def direct_start(n, me, dev, x_ref, recv, send_sem, recv_sem, blk):
    def start(step, carry):
        peer = lax.rem(me + step, n)
        remote(x_ref.at[pl.ds(peer * blk, blk)], recv.at[me], send_sem.at[peer], recv_sem.at[me], dev(peer)).start()
        return carry

    lax.fori_loop(1, n, start, 0)


def direct_finish(n, me, dev, x_ref, out_ref, recv, send_sem, recv_sem, blk):
    out_ref[...] = x_ref[pl.ds(me * blk, blk)]

    def gather(step, carry):
        peer = lax.rem(me + n - step, n)
        remote(x_ref.at[pl.ds(me * blk, blk)], recv.at[peer], send_sem.at[peer], recv_sem.at[peer], dev(peer)).wait_recv()
        out_ref[...] += recv[peer]
        return carry

    lax.fori_loop(1, n, gather, 0)

    def finish(step, carry):
        peer = lax.rem(me + step, n)
        remote(x_ref.at[pl.ds(peer * blk, blk)], recv.at[me], send_sem.at[peer], recv_sem.at[me], dev(peer)).wait_send()
        return carry

    lax.fori_loop(1, n, finish, 0)


def ring_flat(n, me, dev, x_ref, out_ref, recv, sendbuf, send_sem, recv_sem, blk, ready=None, lane_done=None):
    lanes = recv.shape[0]
    part = blk // lanes
    towards = (lax.rem(me + 1, n), lax.rem(me + n - 1, n))

    def chunk_sent(d, step):
        return lax.rem(me - step - 1 + 2 * n, n) if d % 2 == 0 else lax.rem(me + step + 1, n)

    def rows_of(d, chunk):
        return pl.ds(chunk * blk + d * part, part)

    def copy(d, step):
        src = x_ref.at[rows_of(d, chunk_sent(d, 0))] if step == 0 else sendbuf.at[d, step]
        return remote(src, recv.at[d, step], send_sem.at[d, step], recv_sem.at[d, step], dev(towards[d % 2]))

    for d in range(lanes):
        copy(d, 0).start()
    if ready is not None:
        ready()
    for step in range(n - 1):
        for d in range(lanes):
            copy(d, step).wait_recv()
            total = recv[d, step] + x_ref[rows_of(d, chunk_sent(d, step + 1))]
            if step < n - 2:
                sendbuf[d, step + 1] = total
                copy(d, step + 1).start()
            else:
                out_ref[pl.ds(d * part, part)] = total
                if lane_done is not None:
                    lane_done(d, part)
    for step in range(n - 1):
        for d in range(lanes):
            copy(d, step).wait_send()


def ring_phase(n, me, dev, x_ref, out_ref, recv, sendbuf, send_sem, recv_sem):
    right = lax.rem(me + 1, n)
    left = lax.rem(me + n - 1, n)
    half = x_ref.shape[1] // 2
    lanes = (pl.ds(0, half), pl.ds(half, half))
    towards = (right, left)

    def chunk_sent(d, step):
        return lax.rem(me - step - 1 + 2 * n, n) if d == 0 else lax.rem(me + step + 1, n)

    for step in range(n - 1):
        copies = []
        for d in range(2):
            src = x_ref.at[chunk_sent(d, 0), lanes[d]] if step == 0 else sendbuf.at[d, step]
            copy = remote(src, recv.at[d, step], send_sem.at[d, step], recv_sem.at[d, step], dev(towards[d]))
            copy.start()
            copies.append(copy)
        for d in range(2):
            copies[d].wait_recv()
            total = recv[d, step] + x_ref[chunk_sent(d, step + 1), lanes[d]]
            if step < n - 2:
                sendbuf[d, step + 1] = total
            else:
                out_ref[lanes[d]] = total
        for d in range(2):
            copies[d].wait_send()


def whole_kernel(sizes, x_ref, out_ref, core_recv, on_chip, ring_a_recv, ring_a_send, ring_a_out, z_b_recv, z_b_out,
                 z_a_recv, ring_b_recv, ring_b_send, q_buf, gath, gt, terms, recv_col, part, recv_ba, sems):
    n_aa, n_ba, n_y, n_core = sizes
    n_col = n_y * n_core
    per_block = n_ba // n_aa
    out_rows = out_ref.shape[0]
    (s_core, r_core, s_ra, r_ra, s_zb, r_zb, s_za, r_za, s_rb, r_rb, send_g, recv_g, send_c, recv_c, send_b, recv_b) = sems
    me_aa = lax.axis_index("aa")
    me_ba = lax.axis_index("ba")
    me_y = lax.axis_index("y")
    me_core = lax.axis_index("core")
    me_col = me_y * n_core + me_core

    def aa_dev(p):
        return {"aa": p}

    def col_dev(c):
        return {"y": c // n_core, "core": lax.rem(c, n_core)}

    def ba_dev(b):
        return {"ba": b}

    def core_dev(k):
        return {"core": k}

    def y_dev(k):
        return {"y": k}

    barrier = pltpu.get_barrier_semaphore()
    groups = ((n_aa, me_aa, aa_dev), (n_col, me_col, col_dev), (n_ba, me_ba, ba_dev))
    for n, me, dev in groups:
        def greet(step, carry, n=n, me=me, dev=dev):
            pl.semaphore_signal(barrier, inc=1, device_id=dev(lax.rem(me + step, n)), device_id_type=MESH)
            return carry

        lax.fori_loop(1, n, greet, 0)
    pl.semaphore_wait(barrier, n_aa + n_col + n_ba - 3)

    rows_a = on_chip.shape[0] * 3 // 4
    rows_b = on_chip.shape[0] - rows_a
    blk_a = rows_a // n_y
    firsts = sorted({(n_y - 1) % n_y, 1 % n_y})
    offsets = firsts + [o for o in range(n_y) if o not in firsts]
    spans = [pl.ds(lax.rem(me_y + o, n_y) * blk_a, blk_a) for o in offsets] + [pl.ds(rows_a, rows_b)]

    def core_copy(k, src, dst, peer):
        return remote(x_ref.at[src, spans[k]], core_recv.at[dst, spans[k]], s_core.at[k, peer], r_core.at[k, dst],
                      core_dev(peer))

    def core_start(k):
        def start(step, carry):
            peer = lax.rem(me_core + step, n_core)
            core_copy(k, peer, me_core, peer).start()
            return carry

        lax.fori_loop(1, n_core, start, 0)

    def core_finish(k):
        on_chip[spans[k]] = x_ref[me_core, spans[k]]

        def gather(step, carry):
            peer = lax.rem(me_core + n_core - step, n_core)
            core_copy(k, me_core, peer, peer).wait_recv()
            on_chip[spans[k]] += core_recv[peer, spans[k]]
            return carry

        lax.fori_loop(1, n_core, gather, 0)

        def finish(step, carry):
            peer = lax.rem(me_core + step, n_core)
            core_copy(k, peer, me_core, peer).wait_send()
            return carry

        lax.fori_loop(1, n_core, finish, 0)

    for k in [n_y] + list(range(n_y)):
        core_start(k)
    core_finish(n_y)
    part_a = on_chip.at[pl.ds(0, rows_a)]
    part_b = on_chip.at[pl.ds(rows_a, rows_b)]
    blk_zb = rows_b // n_ba
    direct_start(n_ba, me_ba, ba_dev, part_b, z_b_recv, s_zb, r_zb, blk_zb)
    for k in range(len(firsts)):
        core_finish(k)

    def rest_ready():
        for k in range(len(firsts), n_y):
            core_finish(k)

    depth_a = ring_a_out.shape[0] // n_ba

    def send_lane(d, part):
        for p in range(d * part // depth_a, (d + 1) * part // depth_a):
            @pl.when(me_ba != p)
            def _():
                remote(ring_a_out.at[pl.ds(p * depth_a, depth_a)], z_a_recv.at[me_ba], s_za.at[p], r_za.at[me_ba],
                       ba_dev(p)).start()

    ring_flat(n_y, me_y, y_dev, part_a, ring_a_out, ring_a_recv, ring_a_send, s_ra, r_ra, blk_a, ready=rest_ready,
              lane_done=send_lane)
    direct_finish(n_ba, me_ba, ba_dev, part_b, z_b_out, z_b_recv, s_zb, r_zb, blk_zb)
    depth_b = blk_zb // n_y
    ring_flat(n_y, me_y, y_dev, z_b_out, q_buf.at[pl.ds(depth_a, depth_b)], ring_b_recv, ring_b_send, s_rb, r_rb, depth_b)
    direct_finish(n_ba, me_ba, ba_dev, ring_a_out, q_buf.at[pl.ds(0, depth_a)], z_a_recv, s_za, r_za, depth_a)

    q = q_buf[...]
    gath[me_aa] = q

    def g_out(p):
        return remote(q_buf, gath.at[me_aa], send_g.at[p], recv_g.at[me_aa], aa_dev(p))

    def g_in(p):
        return remote(q_buf, gath.at[p], send_g.at[p], recv_g.at[p], aa_dev(p))

    def g_start(step, carry):
        g_out(lax.rem(me_aa + step, n_aa)).start()
        return carry

    lax.fori_loop(1, n_aa, g_start, 0)

    def g_wait(step, carry):
        g_in(lax.rem(me_aa + n_aa - step, n_aa)).wait_recv()
        return carry

    lax.fori_loop(1, n_aa, g_wait, 0)

    def g_done(step, carry):
        g_out(lax.rem(me_aa + step, n_aa)).wait_send()
        return carry

    lax.fori_loop(1, n_aa, g_done, 0)

    for p in range(n_aa):
        gt[p] = gath[p].T

    def term_block(c):
        pieces = []
        for p in range(n_aa):
            for b2 in range(per_block):
                start = pl.multiple_of(b2 * n_col * out_rows + c * out_rows, out_rows)
                pieces.append(gt[p, pl.ds(start, out_rows), :])
        lhs = jnp.concatenate(pieces, axis=0)
        block = jnp.dot(lhs, q, precision=lax.Precision.HIGHEST, preferred_element_type=jnp.float32)
        return block.reshape(n_ba, out_rows, q.shape[1])

    def c_out(c):
        return remote(terms.at[c], recv_col.at[me_col], send_c.at[c], recv_c.at[me_col], col_dev(c))

    def c_in(c):
        return remote(terms.at[me_col], recv_col.at[c], send_c.at[c], recv_c.at[c], col_dev(c))

    def c_start(step, carry):
        c = lax.rem(me_col + step, n_col)
        terms[c] = term_block(c)
        c_out(c).start()
        return carry

    order = sorted(range(1, n_col), key=lambda k: -min(k, n_col - k))
    for step in order:
        c_start(step, 0)
    part[...] = term_block(me_col)

    def c_wait(step, carry):
        peer = lax.rem(me_col + n_col - step, n_col)
        c_in(peer).wait_recv()
        part[...] += recv_col[peer]
        return carry

    lax.fori_loop(1, n_col, c_wait, 0)

    def c_done(step, carry):
        c_out(lax.rem(me_col + step, n_col)).wait_send()
        return carry

    lax.fori_loop(1, n_col, c_done, 0)
    direct_phase(n_ba, me_ba, ba_dev, part, out_ref, recv_ba, send_b, recv_b)


def reduce_and_gram(product, sizes, collective_id):
    n_aa, n_ba, n_y, n_core = sizes
    n_col = n_y * n_core
    depth_all, rows = product.shape
    depth = depth_all // (n_core * n_y * n_ba)
    out_rows = rows * n_aa // (n_ba * n_col)
    rows_c = depth_all // n_core
    rows_a = rows_c * 3 // 4
    blk_a = rows_a // n_y
    blk_zb = (rows_c - rows_a) // n_ba
    depth_a = blk_a // n_ba
    depth_b = blk_zb // n_y
    f32 = jnp.float32
    dma = pltpu.SemaphoreType.DMA
    return pl.pallas_call(
        functools.partial(whole_kernel, sizes),
        out_shape=jax.ShapeDtypeStruct((out_rows, rows), f32),
        in_specs=[pl.BlockSpec(memory_space=pltpu.VMEM)],
        out_specs=pl.BlockSpec(memory_space=pltpu.VMEM),
        scratch_shapes=[
            pltpu.VMEM((n_core, rows_c, rows), f32),
            pltpu.VMEM((rows_c, rows), f32),
            pltpu.VMEM((4, n_y - 1, blk_a // 4, rows), f32),
            pltpu.VMEM((4, n_y - 1, blk_a // 4, rows), f32),
            pltpu.VMEM((blk_a, rows), f32),
            pltpu.VMEM((n_ba, blk_zb, rows), f32),
            pltpu.VMEM((blk_zb, rows), f32),
            pltpu.VMEM((n_ba, depth_a, rows), f32),
            pltpu.VMEM((2, n_y - 1, depth_b // 2, rows), f32),
            pltpu.VMEM((2, n_y - 1, depth_b // 2, rows), f32),
            pltpu.VMEM((depth, rows), f32),
            pltpu.VMEM((n_aa, depth, rows), f32),
            pltpu.VMEM((n_aa, rows, depth), f32),
            pltpu.VMEM((n_col, n_ba, out_rows, rows), f32),
            pltpu.VMEM((n_col, n_ba, out_rows, rows), f32),
            pltpu.VMEM((n_ba, out_rows, rows), f32),
            pltpu.VMEM((n_ba, out_rows, rows), f32),
            [dma((n_y + 1, n_core)), dma((n_y + 1, n_core)), dma((4, n_y - 1)), dma((4, n_y - 1)), dma((n_ba,)), dma((n_ba,)),
             dma((n_ba,)), dma((n_ba,)), dma((2, n_y - 1)), dma((2, n_y - 1)),
             dma((n_aa,)), dma((n_aa,)), dma((n_col,)), dma((n_col,)), dma((n_ba,)), dma((n_ba,))],
        ],
        compiler_params=pltpu.CompilerParams(collective_id=collective_id, has_side_effects=True),
    )(product.reshape(n_core, rows_c, rows))


def project(tensor, factor_two, factor_three):
    rank = factor_three.shape[1]
    local_rows = tensor.shape[0]
    local_two = tensor.shape[1]
    partial_value = jnp.dot(
        tensor.reshape(local_rows * local_two, tensor.shape[2]), factor_three, preferred_element_type=jnp.float32
    ).astype(jnp.bfloat16).reshape(local_rows, local_two, rank)
    product = jnp.einsum("jr,ijs->sri", factor_two, partial_value, preferred_element_type=jnp.float32)
    return product.reshape(rank * rank, local_rows)


def body(tensor, factor_two, factor_three):
    rank = factor_three.shape[1]
    product = project(tensor, factor_two, factor_three)
    sizes = (lax.axis_size("aa"), lax.axis_size("ba"), lax.axis_size("y"), lax.axis_size("core"))
    gram_t = reduce_and_gram(product, sizes, 0)
    return gram_t.T * (1.0 / (rank * rank))
def solution(mesh):
    n_core = 2
    shape = mesh.devices.shape
    split = jax.sharding.Mesh(
        mesh.devices.reshape(shape[0], shape[1], shape[2] // n_core, n_core), ("aa", "ba", "y", "core")
    )
    return jax.shard_map(
        body,
        mesh=split,
        in_specs=(P("aa", "ba", ("y", "core")), P("ba", None), P(("y", "core"), None)),
        out_specs=P("aa", ("ba", "y", "core")),
        check_vma=False,
    )
```

```python
import functools

import jax
import jax.numpy as jnp
from jax import lax
from jax.experimental import pallas as pl
from jax.experimental.pallas import tpu as pltpu
from jax.sharding import PartitionSpec as P

MESH = pl.DeviceIdType.MESH


def remote(src, dst, send, recv, dev):
    return pltpu.make_async_remote_copy(
        src_ref=src, dst_ref=dst, send_sem=send, recv_sem=recv, device_id=dev, device_id_type=MESH
    )


def direct_phase(n, me, dev, x_ref, out_ref, recv, send_sem, recv_sem, blk=None):
    def piece(k):
        return x_ref.at[k] if blk is None else x_ref.at[pl.ds(k * blk, blk)]

    def outgoing(peer):
        return remote(piece(peer), recv.at[me], send_sem.at[peer], recv_sem.at[me], dev(peer))

    def incoming(peer):
        return remote(piece(me), recv.at[peer], send_sem.at[peer], recv_sem.at[peer], dev(peer))

    def start(step, carry):
        outgoing(lax.rem(me + step, n)).start()
        return carry

    for step in sorted(range(1, n), key=lambda k: -min(k, n - k)):
        start(step, 0)
    out_ref[...] = piece(me)[...]

    def gather(step, carry):
        peer = lax.rem(me + n - step, n)
        incoming(peer).wait_recv()
        out_ref[...] += recv[peer]
        return carry

    lax.fori_loop(1, n, gather, 0)

    def finish(step, carry):
        outgoing(lax.rem(me + step, n)).wait_send()
        return carry

    lax.fori_loop(1, n, finish, 0)


def direct_start(n, me, dev, x_ref, recv, send_sem, recv_sem, blk):
    def start(step, carry):
        peer = lax.rem(me + step, n)
        remote(x_ref.at[pl.ds(peer * blk, blk)], recv.at[me], send_sem.at[peer], recv_sem.at[me], dev(peer)).start()
        return carry

    for step in sorted(range(1, n), key=lambda k: -min(k, n - k)):
        start(step, 0)


def direct_finish(n, me, dev, x_ref, out_ref, recv, send_sem, recv_sem, blk):
    out_ref[...] = x_ref[pl.ds(me * blk, blk)]

    def gather(step, carry):
        peer = lax.rem(me + n - step, n)
        remote(x_ref.at[pl.ds(me * blk, blk)], recv.at[peer], send_sem.at[peer], recv_sem.at[peer], dev(peer)).wait_recv()
        out_ref[...] += recv[peer]
        return carry

    lax.fori_loop(1, n, gather, 0)

    def finish(step, carry):
        peer = lax.rem(me + step, n)
        remote(x_ref.at[pl.ds(peer * blk, blk)], recv.at[me], send_sem.at[peer], recv_sem.at[me], dev(peer)).wait_send()
        return carry

    lax.fori_loop(1, n, finish, 0)


def ring_flat(n, me, dev, x_ref, out_ref, recv, sendbuf, send_sem, recv_sem, blk, ready=None, lane_done=None):
    lanes = recv.shape[0]
    part = blk // lanes
    towards = (lax.rem(me + 1, n), lax.rem(me + n - 1, n))

    def chunk_sent(d, step):
        return lax.rem(me - step - 1 + 2 * n, n) if d % 2 == 0 else lax.rem(me + step + 1, n)

    def rows_of(d, chunk):
        return pl.ds(chunk * blk + d * part, part)

    def copy(d, step):
        src = x_ref.at[rows_of(d, chunk_sent(d, 0))] if step == 0 else sendbuf.at[d, step]
        return remote(src, recv.at[d, step], send_sem.at[d, step], recv_sem.at[d, step], dev(towards[d % 2]))

    for d in range(lanes):
        copy(d, 0).start()
    if ready is not None:
        ready()
    for step in range(n - 1):
        for d in range(lanes):
            copy(d, step).wait_recv()
            total = recv[d, step] + x_ref[rows_of(d, chunk_sent(d, step + 1))]
            if step < n - 2:
                sendbuf[d, step + 1] = total
                copy(d, step + 1).start()
            else:
                out_ref[pl.ds(d * part, part)] = total
                if lane_done is not None:
                    lane_done(d, part)
    for step in range(n - 1):
        for d in range(lanes):
            copy(d, step).wait_send()


def ring_phase(n, me, dev, x_ref, out_ref, recv, sendbuf, send_sem, recv_sem):
    right = lax.rem(me + 1, n)
    left = lax.rem(me + n - 1, n)
    half = x_ref.shape[1] // 2
    lanes = (pl.ds(0, half), pl.ds(half, half))
    towards = (right, left)

    def chunk_sent(d, step):
        return lax.rem(me - step - 1 + 2 * n, n) if d == 0 else lax.rem(me + step + 1, n)

    for step in range(n - 1):
        copies = []
        for d in range(2):
            src = x_ref.at[chunk_sent(d, 0), lanes[d]] if step == 0 else sendbuf.at[d, step]
            copy = remote(src, recv.at[d, step], send_sem.at[d, step], recv_sem.at[d, step], dev(towards[d]))
            copy.start()
            copies.append(copy)
        for d in range(2):
            copies[d].wait_recv()
            total = recv[d, step] + x_ref[chunk_sent(d, step + 1), lanes[d]]
            if step < n - 2:
                sendbuf[d, step + 1] = total
            else:
                out_ref[lanes[d]] = total
        for d in range(2):
            copies[d].wait_send()


def whole_kernel(sizes, x_ref, out_ref, core_recv, on_chip, ring_a_recv, ring_a_send, ring_a_out, z_b_recv, z_b_out,
                 z_a_recv, ring_b_recv, ring_b_send, q_buf, gath, gt, terms, recv_col, part, recv_ba, sems):
    n_aa, n_ba, n_y, n_core = sizes
    n_col = n_y * n_core
    per_block = n_ba // n_aa
    out_rows = out_ref.shape[0]
    (s_core, r_core, s_ra, r_ra, s_zb, r_zb, s_za, r_za, s_rb, r_rb, send_g, recv_g, send_c, recv_c, send_b, recv_b) = sems
    me_aa = lax.axis_index("aa")
    me_ba = lax.axis_index("ba")
    me_y = lax.axis_index("y")
    me_core = lax.axis_index("core")
    me_col = me_y * n_core + me_core

    def aa_dev(p):
        return {"aa": p}

    def col_dev(c):
        return {"y": c // n_core, "core": lax.rem(c, n_core)}

    def ba_dev(b):
        return {"ba": b}

    def core_dev(k):
        return {"core": k}

    def y_dev(k):
        return {"y": k}

    barrier = pltpu.get_barrier_semaphore()
    groups = ((n_aa, me_aa, aa_dev), (n_col, me_col, col_dev), (n_ba, me_ba, ba_dev))
    for n, me, dev in groups:
        def greet(step, carry, n=n, me=me, dev=dev):
            pl.semaphore_signal(barrier, inc=1, device_id=dev(lax.rem(me + step, n)), device_id_type=MESH)
            return carry

        lax.fori_loop(1, n, greet, 0)
    pl.semaphore_wait(barrier, n_aa + n_col + n_ba - 3)

    rows_a = on_chip.shape[0] * 3 // 4
    rows_b = on_chip.shape[0] - rows_a
    blk_a = rows_a // n_y
    firsts = sorted({(n_y - 1) % n_y, 1 % n_y})
    offsets = firsts + [o for o in range(n_y) if o not in firsts]
    spans = [pl.ds(lax.rem(me_y + o, n_y) * blk_a, blk_a) for o in offsets] + [pl.ds(rows_a, rows_b)]

    def core_copy(k, src, dst, peer):
        return remote(x_ref.at[src, spans[k]], core_recv.at[dst, spans[k]], s_core.at[k, peer], r_core.at[k, dst],
                      core_dev(peer))

    def core_start(k):
        def start(step, carry):
            peer = lax.rem(me_core + step, n_core)
            core_copy(k, peer, me_core, peer).start()
            return carry

        lax.fori_loop(1, n_core, start, 0)

    def core_finish(k):
        on_chip[spans[k]] = x_ref[me_core, spans[k]]

        def gather(step, carry):
            peer = lax.rem(me_core + n_core - step, n_core)
            core_copy(k, me_core, peer, peer).wait_recv()
            on_chip[spans[k]] += core_recv[peer, spans[k]]
            return carry

        lax.fori_loop(1, n_core, gather, 0)

        def finish(step, carry):
            peer = lax.rem(me_core + step, n_core)
            core_copy(k, peer, me_core, peer).wait_send()
            return carry

        lax.fori_loop(1, n_core, finish, 0)

    for k in [n_y] + list(range(n_y)):
        core_start(k)
    core_finish(n_y)
    part_a = on_chip.at[pl.ds(0, rows_a)]
    part_b = on_chip.at[pl.ds(rows_a, rows_b)]
    blk_zb = rows_b // n_ba
    direct_start(n_ba, me_ba, ba_dev, part_b, z_b_recv, s_zb, r_zb, blk_zb)
    for k in range(len(firsts)):
        core_finish(k)

    def rest_ready():
        for k in range(len(firsts), n_y):
            core_finish(k)

    depth_a = ring_a_out.shape[0] // n_ba

    def send_lane(d, part):
        for p in range(d * part // depth_a, (d + 1) * part // depth_a):
            @pl.when(me_ba != p)
            def _():
                remote(ring_a_out.at[pl.ds(p * depth_a, depth_a)], z_a_recv.at[me_ba], s_za.at[p], r_za.at[me_ba],
                       ba_dev(p)).start()

    ring_flat(n_y, me_y, y_dev, part_a, ring_a_out, ring_a_recv, ring_a_send, s_ra, r_ra, blk_a, ready=rest_ready,
              lane_done=send_lane)
    direct_finish(n_ba, me_ba, ba_dev, part_b, z_b_out, z_b_recv, s_zb, r_zb, blk_zb)
    depth_b = blk_zb // n_y
    ring_flat(n_y, me_y, y_dev, z_b_out, q_buf.at[pl.ds(depth_a, depth_b)], ring_b_recv, ring_b_send, s_rb, r_rb, depth_b)
    direct_finish(n_ba, me_ba, ba_dev, ring_a_out, q_buf.at[pl.ds(0, depth_a)], z_a_recv, s_za, r_za, depth_a)

    q = q_buf[...]
    gath[me_aa] = q

    def g_out(p):
        return remote(q_buf, gath.at[me_aa], send_g.at[p], recv_g.at[me_aa], aa_dev(p))

    def g_in(p):
        return remote(q_buf, gath.at[p], send_g.at[p], recv_g.at[p], aa_dev(p))

    def g_start(step, carry):
        g_out(lax.rem(me_aa + step, n_aa)).start()
        return carry

    lax.fori_loop(1, n_aa, g_start, 0)

    def g_wait(step, carry):
        g_in(lax.rem(me_aa + n_aa - step, n_aa)).wait_recv()
        return carry

    lax.fori_loop(1, n_aa, g_wait, 0)

    def g_done(step, carry):
        g_out(lax.rem(me_aa + step, n_aa)).wait_send()
        return carry

    lax.fori_loop(1, n_aa, g_done, 0)

    for p in range(n_aa):
        gt[p] = gath[p].T

    def term_block(c):
        pieces = []
        for p in range(n_aa):
            for b2 in range(per_block):
                start = pl.multiple_of(b2 * n_col * out_rows + c * out_rows, out_rows)
                pieces.append(gt[p, pl.ds(start, out_rows), :])
        lhs = jnp.concatenate(pieces, axis=0)
        block = jnp.dot(lhs, q, precision=lax.Precision.HIGHEST, preferred_element_type=jnp.float32)
        return block.reshape(n_ba, out_rows, q.shape[1])

    def c_out(c):
        return remote(terms.at[c], recv_col.at[me_col], send_c.at[c], recv_c.at[me_col], col_dev(c))

    def c_in(c):
        return remote(terms.at[me_col], recv_col.at[c], send_c.at[c], recv_c.at[c], col_dev(c))

    def c_start(step, carry):
        c = lax.rem(me_col + step, n_col)
        terms[c] = term_block(c)
        c_out(c).start()
        return carry

    order = sorted(range(1, n_col), key=lambda k: -min(k, n_col - k))
    for step in order:
        c_start(step, 0)
    part[...] = term_block(me_col)

    def c_wait(step, carry):
        peer = lax.rem(me_col + n_col - step, n_col)
        c_in(peer).wait_recv()
        part[...] += recv_col[peer]
        return carry

    lax.fori_loop(1, n_col, c_wait, 0)

    def c_done(step, carry):
        c_out(lax.rem(me_col + step, n_col)).wait_send()
        return carry

    lax.fori_loop(1, n_col, c_done, 0)
    direct_phase(n_ba, me_ba, ba_dev, part, out_ref, recv_ba, send_b, recv_b)


def reduce_and_gram(product, sizes, collective_id):
    n_aa, n_ba, n_y, n_core = sizes
    n_col = n_y * n_core
    depth_all, rows = product.shape
    depth = depth_all // (n_core * n_y * n_ba)
    out_rows = rows * n_aa // (n_ba * n_col)
    rows_c = depth_all // n_core
    rows_a = rows_c * 3 // 4
    blk_a = rows_a // n_y
    blk_zb = (rows_c - rows_a) // n_ba
    depth_a = blk_a // n_ba
    depth_b = blk_zb // n_y
    f32 = jnp.float32
    dma = pltpu.SemaphoreType.DMA
    return pl.pallas_call(
        functools.partial(whole_kernel, sizes),
        out_shape=jax.ShapeDtypeStruct((out_rows, rows), f32),
        in_specs=[pl.BlockSpec(memory_space=pltpu.VMEM)],
        out_specs=pl.BlockSpec(memory_space=pltpu.VMEM),
        scratch_shapes=[
            pltpu.VMEM((n_core, rows_c, rows), f32),
            pltpu.VMEM((rows_c, rows), f32),
            pltpu.VMEM((4, n_y - 1, blk_a // 4, rows), f32),
            pltpu.VMEM((4, n_y - 1, blk_a // 4, rows), f32),
            pltpu.VMEM((blk_a, rows), f32),
            pltpu.VMEM((n_ba, blk_zb, rows), f32),
            pltpu.VMEM((blk_zb, rows), f32),
            pltpu.VMEM((n_ba, depth_a, rows), f32),
            pltpu.VMEM((2, n_y - 1, depth_b // 2, rows), f32),
            pltpu.VMEM((2, n_y - 1, depth_b // 2, rows), f32),
            pltpu.VMEM((depth, rows), f32),
            pltpu.VMEM((n_aa, depth, rows), f32),
            pltpu.VMEM((n_aa, rows, depth), f32),
            pltpu.VMEM((n_col, n_ba, out_rows, rows), f32),
            pltpu.VMEM((n_col, n_ba, out_rows, rows), f32),
            pltpu.VMEM((n_ba, out_rows, rows), f32),
            pltpu.VMEM((n_ba, out_rows, rows), f32),
            [dma((n_y + 1, n_core)), dma((n_y + 1, n_core)), dma((4, n_y - 1)), dma((4, n_y - 1)), dma((n_ba,)), dma((n_ba,)),
             dma((n_ba,)), dma((n_ba,)), dma((2, n_y - 1)), dma((2, n_y - 1)),
             dma((n_aa,)), dma((n_aa,)), dma((n_col,)), dma((n_col,)), dma((n_ba,)), dma((n_ba,))],
        ],
        compiler_params=pltpu.CompilerParams(collective_id=collective_id, has_side_effects=True),
    )(product.reshape(n_core, rows_c, rows))


def project(tensor, factor_two, factor_three):
    rank = factor_three.shape[1]
    local_rows = tensor.shape[0]
    local_two = tensor.shape[1]
    partial_value = jnp.dot(
        tensor.reshape(local_rows * local_two, tensor.shape[2]), factor_three, preferred_element_type=jnp.float32
    ).astype(jnp.bfloat16).reshape(local_rows, local_two, rank)
    product = jnp.einsum("jr,ijs->sri", factor_two, partial_value, preferred_element_type=jnp.float32)
    return product.reshape(rank * rank, local_rows)


def body(tensor, factor_two, factor_three):
    rank = factor_three.shape[1]
    product = project(tensor, factor_two, factor_three)
    sizes = (lax.axis_size("aa"), lax.axis_size("ba"), lax.axis_size("y"), lax.axis_size("core"))
    gram_t = reduce_and_gram(product, sizes, 0)
    return gram_t.T * (1.0 / (rank * rank))
def solution(mesh):
    n_core = 2
    shape = mesh.devices.shape
    split = jax.sharding.Mesh(
        mesh.devices.reshape(shape[0], shape[1], shape[2] // n_core, n_core), ("aa", "ba", "y", "core")
    )
    return jax.shard_map(
        body,
        mesh=split,
        in_specs=(P("aa", "ba", ("y", "core")), P("ba", None), P(("y", "core"), None)),
        out_specs=P("aa", ("ba", "y", "core")),
        check_vma=False,
    )
```
